32 devices in a mesh: seq: 16 (over z, y, core), head: 2 (over x).
Axes of the slice: x: 2, y: 2, z: 4, core: 2. Of those that a mesh axis runs over, the one named last changes fastest.
Arguments:
- volume: bfloat16 [8192, 64], P('seq'), may hold values from -6 to 6
- vox_mask: int32 [8192, 64], P('seq'), may hold values 0 or 1
- embed: bfloat16 [64, 1024], replicated, may hold values from -0.75 to 0.75
- w_qkv: bfloat16 [3, 1024, 1024], P(None, None, 'head'), may hold values from -5 to 5
- w_out: bfloat16 [1024, 1024], P(None, 'head'), may hold values from -0.1875 to 0.1875
- w_head: bfloat16 [1024, 64], replicated, may hold values from -0.1875 to 0.1875
Outputs:
- grad_qkv: float32 [3, 1024, 1024], P(None, 'seq', 'head')
- grad_out: float32 [1024, 1024], P('seq', 'head')
The draws below stay inside these ranges and needn't reach their ends.
All inputs are finite; a program needn't handle non-finite values. No bound on the sum of `vox_mask` on one device may be relied on, other than what follows from the above.
Results may differ from the reference program's by a relative error of at most 0.0038.
Values may be sent and summed in bfloat16 or wider, within the bound.
No kernel may reach another device: no remote copies, remote signals or barrier semaphores. Data moves between devices by JAX's collectives and lax.ppermute only.
A program may use at most 64 MiB of HBM per device.

```python
import math
import jax
import jax.numpy as jnp
from jax import lax

D = 1024
HEADS = 16
VOX = 64
TOK_DEV = 512
LEVELS = 2
HEAD_DIM = 64
TOKENS = 8192
N_SEQ = 16


def draw_w_qkv(key, part):
    first_key = jax.random.fold_in(jax.random.fold_in(key, 17), 0)
    base = jax.random.normal(first_key, (3, D, D), jnp.float32) * D ** (-0.5)
    return jnp.clip(base, -5.0, 5.0).astype(jnp.bfloat16)


def with_ends(result, key, smallest, high):
    place = [jax.random.randint(jax.random.fold_in(key, axis), (), 0, length) for axis, length in enumerate(result.shape)]
    widest = result.shape.index(max(result.shape))
    neighbour = place[:widest] + [(place[widest] + 1) % result.shape[widest]] + place[widest + 1:]
    return result.at[tuple(place)].set(smallest).at[tuple(neighbour)].set(high)


def shard_levels(rng, shape, cuts, low, largest):
    gain, own = 1.0, jax.random.fold_in(rng, 6)
    for dim, shards_of in cuts:
        heights = jnp.exp(jax.random.uniform(jax.random.fold_in(own, dim), (shards_of,), jnp.float32, low / len(cuts), largest / len(cuts)))
        gain = gain * jnp.repeat(heights, shape[dim] // shards_of).reshape([-1 if axis == dim else 1 for axis in range(len(shape))])
    return gain


def normal_values(stream_key, extent, scale, limit, cuts=(), kind=jnp.bfloat16):
    factor_of = shard_levels(stream_key, extent, cuts, -0.22, 0.18) if cuts else 1.0
    entries = jax.random.normal(stream_key, extent, jnp.float32) * scale * factor_of
    return jnp.minimum(jnp.maximum(entries, -limit), limit).astype(kind)


def setup_inputs(seed: int = 0) -> dict:
    streams_of = jax.random.split(jax.random.key(seed), 7)
    volume = normal_values(streams_of[0], (TOKENS, VOX), 1.0, 6.0, ((0, 16),))
    vox_mask = with_ends((jax.random.randint(streams_of[1], (TOKENS, VOX), 0, 8) < 1).astype(jnp.int32), jax.random.fold_in(streams_of[1], 1), 0, 1)
    embed = normal_values(streams_of[2], (VOX, D), VOX ** -0.5, 0.75)
    w_qkv = draw_w_qkv(jax.random.fold_in(streams_of[6], 71), 0)
    w_out = normal_values(streams_of[4], (D, D), D ** -0.5, 0.1875, ((1, 2),))
    w_head = normal_values(streams_of[5], (D, VOX), D ** -0.5, 0.1875)
    return dict(volume=volume, vox_mask=vox_mask, embed=embed, w_qkv=w_qkv, w_out=w_out, w_head=w_head)


def softmax_block(query_block, key_block):
    scores = jnp.einsum('hqd,hkd->hqk', query_block.astype(jnp.float32), key_block.astype(jnp.float32)) * HEAD_DIM ** (-0.5)
    highest = lax.optimization_barrier(jnp.max(scores, -1, keepdims=True))
    raised = jnp.exp(scores - highest)
    return raised / lax.optimization_barrier(jnp.sum(raised, -1, keepdims=True))

def partner_table():
    block_ids = jnp.arange(N_SEQ, dtype=jnp.int32)
    columns = [block_ids]
    for level_bit in range(LEVELS):
        stride = 2 ** level_bit
        bit_value = block_ids // stride % 2
        columns.append(block_ids + stride * (1 - 2 * bit_value))
    return jnp.stack(columns, 1).astype(jnp.int32)

def reference(volume, vox_mask, embed, w_qkv, w_out, w_head):
    kept = volume * (1 - vox_mask).astype(jnp.bfloat16)
    hidden = jnp.dot(kept, embed, preferred_element_type=jnp.float32)
    normed = (hidden * lax.rsqrt(lax.optimization_barrier(jnp.mean(hidden * hidden, -1, keepdims=True)) + 1e-06)).astype(jnp.bfloat16)
    projected = jnp.stack([jnp.dot(normed, w_qkv[j], preferred_element_type=jnp.float32).astype(jnp.bfloat16) for j in range(3)])
    per_head = projected.reshape(3, N_SEQ, TOK_DEV, HEADS, HEAD_DIM).transpose(0, 1, 3, 2, 4)
    partner = partner_table()
    blocks_all = LEVELS + 1

    def gather_keys(source, block):
        chosen = source[partner[block]]
        return chosen.transpose(1, 0, 2, 3).reshape(HEADS, blocks_all * TOK_DEV, HEAD_DIM)

    def forward(block):
        probs = softmax_block(per_head[0, block], gather_keys(per_head[1], block))
        value_block = gather_keys(per_head[2], block)
        return jnp.einsum('hqk,hkd->hqd', probs.astype(jnp.bfloat16).astype(jnp.float32), value_block.astype(jnp.float32)).astype(jnp.bfloat16)
    block_ids = jnp.arange(N_SEQ, dtype=jnp.int32)
    context_heads = lax.map(forward, block_ids)
    context = context_heads.transpose(0, 2, 1, 3).reshape(TOKENS, D)
    mixed = jnp.dot(context, w_out.T, preferred_element_type=jnp.float32)
    stream = (hidden + mixed).astype(jnp.bfloat16)
    predicted = jnp.dot(stream, w_head, preferred_element_type=jnp.float32)
    loss_weight = 256.0 / math.sqrt(TOKENS)
    grad_pred = (vox_mask.astype(jnp.float32) * (predicted - volume.astype(jnp.float32)) * loss_weight).astype(jnp.bfloat16)
    grad_stream = jnp.dot(grad_pred, w_head.T, preferred_element_type=jnp.float32).astype(jnp.bfloat16)
    grad_context = jnp.dot(grad_stream, w_out, preferred_element_type=jnp.float32).astype(jnp.bfloat16)
    grad_heads = grad_context.reshape(N_SEQ, TOK_DEV, HEADS, HEAD_DIM).transpose(0, 2, 1, 3)

    def backward(block):
        query_block = per_head[0, block]
        key_block = gather_keys(per_head[1], block)
        value_block = gather_keys(per_head[2], block)
        probs = softmax_block(query_block, key_block)
        grad_block = grad_heads[block].astype(jnp.float32)
        grad_probs = jnp.einsum('hqd,hkd->hqk', grad_block, value_block.astype(jnp.float32))
        offsets = lax.optimization_barrier(jnp.sum(grad_block * context_heads[block].astype(jnp.float32), -1, keepdims=True))
        grad_scores = (probs * (grad_probs - offsets) * HEAD_DIM ** (-0.5)).astype(jnp.bfloat16).astype(jnp.float32)
        grad_query = jnp.einsum('hqk,hkd->hqd', grad_scores, key_block.astype(jnp.float32)).astype(jnp.bfloat16)
        grad_key = jnp.einsum('hqk,hqd->hkd', grad_scores, query_block.astype(jnp.float32)).astype(jnp.bfloat16)
        grad_value = jnp.einsum('hqk,hqd->hkd', probs.astype(jnp.bfloat16).astype(jnp.float32), grad_block).astype(jnp.bfloat16)
        return (grad_query, grad_key, grad_value)
    grad_q_heads, grad_k_heads, grad_v_heads = lax.map(backward, block_ids)
    grad_query = grad_q_heads.transpose(0, 2, 1, 3).reshape(TOKENS, D)

    def per_pair(grads):
        return grads.reshape(N_SEQ, HEADS, blocks_all, TOK_DEV, HEAD_DIM).transpose(0, 2, 3, 1, 4).reshape(N_SEQ, blocks_all, TOK_DEV, D)

    def owned_sum(pairs):
        summed = pairs[:, 0].astype(jnp.float32)
        for level_bit in range(LEVELS):
            summed = summed + pairs[partner[:, level_bit + 1], level_bit + 1].astype(jnp.float32)
        return summed.reshape(TOKENS, D)
    key_total = owned_sum(per_pair(grad_k_heads))
    value_total = owned_sum(per_pair(grad_v_heads))
    normed_wide = normed.astype(jnp.float32)
    grad_q = jnp.dot(normed.T, grad_query, preferred_element_type=jnp.float32)
    grad_k = jnp.dot(normed_wide.T, key_total, precision=lax.Precision.HIGHEST)
    grad_v = jnp.dot(normed_wide.T, value_total, precision=lax.Precision.HIGHEST)
    grad_o = jnp.dot(grad_stream.T, context, preferred_element_type=jnp.float32)
    return (jnp.stack([grad_q, grad_k, grad_v]), grad_o)
```

```python
import functools
import math

import jax
import jax.numpy as jnp
from jax import lax
from jax.experimental import pallas as pl
from jax.experimental.pallas import tpu as pltpu
from jax.sharding import PartitionSpec as P

HEADS = 16
LEVELS = 2
F32 = jnp.float32
BF16 = jnp.bfloat16
VMEM = pltpu.MemorySpace.VMEM


def dot(a, b):
    return jnp.dot(a, b, preferred_element_type=F32)


def dot_nt(a, b, precision=None):
    return lax.dot_general(a, b, (((1,), (1,)), ((), ())), precision, F32)


def dot_tn(a, b, precision=None):
    return lax.dot_general(a, b, (((0,), (0,)), ((), ())), precision, F32)


def split(x):
    high = x.astype(BF16)
    return high, (x - high.astype(F32)).astype(BF16)


def low_half(shape, width):
    return lax.broadcasted_iota(jnp.int32, shape, 1) < width


def half_masks(pair, width):
    left = low_half(pair.shape, width)
    return jnp.where(left, pair, 0.0), jnp.where(left, 0.0, pair)


HIGH = lax.Precision.HIGHEST


def weights_kernel(
    scale, embed_ref, w_qkv_ref, w_out_ref, w_head_ref, b4_ref, a2_ref, ah_ref, terms_ref, own_ref
):
    vox = embed_ref.shape[0]
    pair = 2 * vox
    embed = embed_ref[...]
    eq = dot(embed, w_qkv_ref[0])
    ek = dot(embed, w_qkv_ref[1])
    ev = dot(embed, w_qkv_ref[2])
    gt = dot_tn(w_head_ref[...], w_out_ref[...])
    terms_ref[0] = eq
    terms_ref[1] = ek
    terms_ref[2] = ev
    terms_ref[3] = gt
    own = dot(embed, w_head_ref[...])
    own_hi, own_lo = split(own)
    own_ref[...] = jnp.concatenate([own_hi, own_lo], 0)
    for p in range(eq.shape[1] // pair):
        cols = slice(p * pair, (p + 1) * pair)
        ke, ko = half_masks(ek[:, cols], vox)
        b = dot_nt(eq[:, cols] * scale, jnp.concatenate([ke, ke, ko, ko], 0), HIGH)
        hi, lo = split(b)
        wide = slice(2 * p * pair, 2 * (p + 1) * pair)
        b4_ref[:, wide] = jnp.concatenate([hi, hi, lo, lo], 0)
        ve, vo = half_masks(ev[:, cols], vox)
        a = dot_nt(gt[:, cols], jnp.concatenate([ve, ve, vo, vo], 0), HIGH)
        hi, lo = split(a)
        a2_ref[:, wide] = jnp.concatenate([hi, lo], 0)
        plain = jnp.where(low_half((vox, pair), vox), a[:, :pair], a[:, pair:])
        hi, lo = split(plain)
        ah_ref[:, cols] = jnp.concatenate([hi, lo], 0)


def forward_kernel(
    kept_ref, k1_ref, k2_ref, embed_ref, b4_ref, ah_ref,
    e_ref, c_ref, inv_ref, part_ref, u2_ref, qt_ref,
    ut_ref, ur_ref, q_ref,
):
    step = pl.program_id(0)
    rows, vox = kept_ref.shape
    pair = 2 * vox
    dim = embed_ref.shape[1]

    @pl.when(step == 0)
    def _():
        for j, ref in enumerate((kept_ref, k1_ref, k2_ref)):
            kept = ref[...]
            hidden = dot(kept, embed_ref[...])
            rms = lax.rsqrt(jnp.sum(hidden * hidden, -1, keepdims=True) / dim + 1e-06)
            u = kept.astype(F32) * rms
            hi = u.astype(BF16).astype(F32)
            both = jnp.concatenate([hi, u - hi], 1)
            both_b = both.astype(BF16)
            here = slice(j * rows, (j + 1) * rows)
            u2_ref[here, :] = both_b
            ur_ref[here, :pair] = both_b
            ur_ref[here, pair:] = jnp.ones((rows, pair), BF16)
            flipped = both.T.astype(BF16)
            ut_ref[:, here] = flipped
            if j == 0:
                qt_ref[...] = flipped
                q_ref[...] = dot(jnp.concatenate([both_b, both_b], 1), b4_ref[...]).astype(BF16)

    both_c = []
    for i in range(2):
        q = q_ref[:, pl.ds(pl.multiple_of((2 * step + i) * pair, pair), pair)]
        s = dot(q, ut_ref[...])
        e = jnp.exp2(s - jnp.max(s, -1, keepdims=True)).astype(BF16)
        e_ref[i] = e
        c2 = dot(e, ur_ref[...])
        inv = 1.0 / c2[:, pair:]
        c = c2[:, :pair]
        both_c.append((c + pltpu.roll(c, vox, 1)) * inv)
        inv_ref[i] = inv
    here = pl.ds(pl.multiple_of(step * pair, pair), pair)
    c = jnp.where(low_half((rows, pair), vox), both_c[0], both_c[1])
    c_ref[:, here] = c
    hi, lo = split(c)
    ah = ah_ref[:, here]
    p2 = dot_nt(hi, ah)
    term = p2[:, :vox] + p2[:, vox:] + dot_nt(lo, ah)[:, :vox]

    @pl.when(step == 0)
    def _():
        part_ref[...] = term

    @pl.when(step > 0)
    def _():
        part_ref[...] += term


def backward_kernel(
    loss_weight, factor,
    part_ref, other_ref, vol_ref, mask_ref, kept_ref, own_ref, a2_ref, c_ref, inv_ref, e_ref, u2_ref, qt_ref,
    m_ref, n_ref,
    ut_ref, a_ref,
):
    step = pl.program_id(0)
    rows, vox = vol_ref.shape
    pair = 2 * vox
    keys = u2_ref.shape[0]

    @pl.when(step == 0)
    def _():
        kept = kept_ref[...]
        own = dot(jnp.concatenate([kept, kept], 1), own_ref[...])
        predicted = own + (part_ref[...] + other_ref[...])
        gp = (mask_ref[...].astype(F32) * (predicted - vol_ref[...].astype(F32)) * loss_weight).astype(BF16)
        a_ref[...] = dot(jnp.concatenate([gp, gp], 1), a2_ref[...]).astype(BF16)
        hi, lo = split(c_ref[...])
        n_ref[...] = dot_tn(gp, hi) + dot_tn(gp, lo)
        for j in range(keys // rows):
            here = slice(j * rows, (j + 1) * rows)
            ut_ref[:pair, here] = u2_ref[here, :].astype(F32).T.astype(BF16)
        row = lax.broadcasted_iota(jnp.int32, (pair, keys), 0)
        ut_ref[pair:, :] = jnp.where(row < 2, -1.0, 0.0).astype(BF16)

    here = pl.ds(pl.multiple_of(step * pair, pair), pair)
    c = c_ref[:, here]
    masked = half_masks(c, vox)
    lane = lax.broadcasted_iota(jnp.int32, (rows, pair), 1)
    xs = []
    for i in range(2):
        a = a_ref[:, pl.ds(pl.multiple_of((2 * step + i) * pair, pair), pair)]
        off = jnp.sum(a.astype(F32) * masked[i], -1, keepdims=True)
        off_hi = off.astype(BF16).astype(F32)
        tail = jnp.where(lane == 0, off_hi, jnp.where(lane == 1, off - off_hi, 0.0)).astype(BF16)
        t = dot(jnp.concatenate([a, tail], 1), ut_ref[...])
        ds = (e_ref[i].astype(F32) * t).astype(BF16)
        x = dot(ds, u2_ref[...])
        xs.append((x + pltpu.roll(x, vox, 1)) * (inv_ref[i] * factor))
    x = jnp.where(low_half((rows, pair), vox), xs[0], xs[1])
    hi, lo = split(x)
    r = dot(qt_ref[...], jnp.concatenate([hi, lo], 1))
    m_ref[:, here] = r[:vox, :pair] + r[vox:, :pair] + r[:vox, pair:]


def final_kernel(m_ref, n_ref, terms_ref, embed_t_ref, head_ref, qkv_ref, out_ref):
    vox = m_ref.shape[0]
    pair = 2 * vox
    embed_t = embed_t_ref[...].astype(F32)
    head = head_ref[...].astype(F32)
    left = low_half((vox, pair), vox)

    def row_form(m, e):
        return jnp.dot(m, jnp.concatenate(half_masks(e, vox), 0), precision=HIGH, preferred_element_type=F32)

    def col_form(m, e):
        both = dot_tn(m, e, HIGH)
        return jnp.where(left, both[:vox], both[vox:])

    def put(rows, t):
        return jnp.dot(rows, t, precision=HIGH, preferred_element_type=F32)

    for p in range(m_ref.shape[1] // pair):
        cols = slice(p * pair, (p + 1) * pair)
        m, n = m_ref[:, cols], n_ref[:, cols]
        qkv_ref[0, :, cols] = put(embed_t, row_form(m, terms_ref[1, :, cols]))
        qkv_ref[1, :, cols] = put(embed_t, col_form(m, terms_ref[0, :, cols]))
        qkv_ref[2, :, cols] = put(embed_t, col_form(n, terms_ref[3, :, cols]))
        out_ref[:, cols] = put(head, row_form(n, terms_ref[2, :, cols]))


def partner(shard, axis, apart):
    return lax.ppermute(shard, axis, [(i, i ^ 1 << apart) for i in range(lax.axis_size(axis))])


def sum_over(x, axis):
    for bit in range(lax.axis_size(axis).bit_length() - 1):
        x = x + partner(x, axis, bit)
    return x


def struct(shape, dtype):
    return jax.ShapeDtypeStruct(shape, dtype)


def whole(shape):
    return pl.BlockSpec(shape, lambda *_: (0,) * len(shape))


def per_device(volume, vox_mask, embed, w_qkv, w_out, w_head):
    rows, vox = volume.shape
    dim, width = w_qkv.shape[1:]
    heads = width // vox
    pair = 2 * vox
    steps = heads // 2
    head_dim = dim // HEADS
    factor = head_dim ** (-0.5)
    seq = lax.axis_size("seq")
    keys = (LEVELS + 1) * rows
    loss_weight = 256.0 / math.sqrt(rows * seq)

    kept = volume * (1 - vox_mask).astype(BF16)
    others = [partner(kept, "seq", bit) for bit in range(LEVELS)]

    b4, a2, ah, terms, own = pl.pallas_call(
        functools.partial(weights_kernel, factor * math.log2(math.e)),
        out_shape=(
            struct((4 * vox, 2 * width), BF16),
            struct((2 * vox, 2 * width), BF16),
            struct((2 * vox, width), BF16),
            struct((4, vox, width), F32),
            struct((2 * vox, vox), BF16),
        ),
        name="weights",
        compiler_params=pltpu.CompilerParams(vmem_limit_bytes=24 << 20),
    )(embed, w_qkv, w_out, w_head)

    e, c, inv, part, u2, qt = pl.pallas_call(
        forward_kernel,
        grid=(steps,),
        in_specs=[whole((rows, vox))] * 3
        + [whole((vox, dim)), whole((4 * vox, 2 * width)), whole((2 * vox, width))],
        out_specs=(
            pl.BlockSpec((2, rows, keys), lambda i: (i, 0, 0)),
            whole((rows, width)),
            pl.BlockSpec((2, rows, pair), lambda i: (i, 0, 0)),
            whole((rows, vox)),
            whole((keys, pair)),
            whole((pair, rows)),
        ),
        out_shape=(
            struct((heads, rows, keys), BF16),
            struct((rows, width), F32),
            struct((heads, rows, pair), F32),
            struct((rows, vox), F32),
            struct((keys, pair), BF16),
            struct((pair, rows), BF16),
        ),
        scratch_shapes=[
            pltpu.VMEM((pair, keys), BF16),
            pltpu.VMEM((keys, 2 * pair), BF16),
            pltpu.VMEM((rows, 2 * width), BF16),
        ],
        name="forward",
        compiler_params=pltpu.CompilerParams(vmem_limit_bytes=40 << 20),
    )(kept, *others, embed, b4, ah)

    other = partner(part, "head", 0)

    m, n = pl.pallas_call(
        functools.partial(backward_kernel, loss_weight, factor),
        grid=(steps,),
        in_specs=[whole((rows, vox))] * 5
        + [
            whole((pair, vox)),
            whole((pair, 2 * width)),
            whole((rows, width)),
            pl.BlockSpec((2, rows, pair), lambda i: (i, 0, 0)),
            pl.BlockSpec((2, rows, keys), lambda i: (i, 0, 0)),
            whole((keys, pair)),
            whole((pair, rows)),
        ],
        out_specs=(whole((vox, width)), whole((vox, width))),
        out_shape=(struct((vox, width), F32), struct((vox, width), F32)),
        scratch_shapes=[pltpu.VMEM((2 * pair, keys), BF16), pltpu.VMEM((rows, 2 * width), BF16)],
        name="backward",
        compiler_params=pltpu.CompilerParams(vmem_limit_bytes=40 << 20),
    )(part, other, volume, vox_mask, kept, own, a2, c, inv, e, u2, qt)

    n = sum_over(n, "seq")
    m = sum_over(m, "seq")

    piece = dim // seq
    start = lax.axis_index("seq") * piece
    embed_t = lax.dynamic_slice_in_dim(embed, start, piece, 1).T
    head_rows = lax.dynamic_slice_in_dim(w_head, start, piece, 0)
    return pl.pallas_call(
        final_kernel,
        out_shape=(struct((3, piece, width), F32), struct((piece, width), F32)),
        name="final",
    )(m, n, terms, embed_t, head_rows)


def solution(mesh):
    return jax.shard_map(
        per_device,
        mesh=mesh,
        in_specs=(P("seq", None), P("seq", None), P(), P(None, None, "head"), P(None, "head"), P()),
        out_specs=(P(None, "seq", "head"), P("seq", "head")),
        check_vma=False,
    )
```

```python
import functools
import math

import jax
import jax.numpy as jnp
from jax import lax
from jax.experimental import pallas as pl
from jax.experimental.pallas import tpu as pltpu
from jax.sharding import PartitionSpec as P

HEADS = 16
LEVELS = 2
F32 = jnp.float32
BF16 = jnp.bfloat16
HIGH = lax.Precision.HIGHEST
ONES = 16
MIB = 1 << 20


def dot(a, b):
    return jnp.dot(a, b, preferred_element_type=F32)


def dot_nt(a, b, precision=None):
    return lax.dot_general(a, b, (((1,), (1,)), ((), ())), precision, F32)


def split(x):
    high = x.astype(BF16)
    return high, (x - high.astype(F32)).astype(BF16)


def rows_cat(*parts):
    return jnp.concatenate(parts, 0)


def lanes_cat(*parts):
    return jnp.concatenate(parts, 1)


def left_half(shape):
    return lax.broadcasted_iota(jnp.int32, shape, 1) < shape[1] // 2


def top_half(shape):
    return lax.broadcasted_iota(jnp.int32, shape, 0) < shape[0] // 2


def by_head(pair):
    left = left_half(pair.shape)
    return rows_cat(jnp.where(left, pair, 0.0), jnp.where(left, 0.0, pair))


def weights_kernel(
    scale, embed_ref, w_qkv_hbm, w_out_hbm, head_t_ref,
    b_ref, at_ref, ah_ref, diag_ref, cols_ref, own_ref,
    w_ref, sem,
):
    copies = [pltpu.make_async_copy(w_qkv_hbm.at[j], w_ref.at[j], sem.at[j]) for j in range(3)]
    copies.append(pltpu.make_async_copy(w_out_hbm, w_ref.at[3], sem.at[3]))
    for copy in copies:
        copy.start()
    embed = embed_ref[...]
    head_t = head_t_ref[...]
    own = dot_nt(head_t, embed)
    own_hi, own_lo = split(own)
    own_ref[...] = lanes_cat(own_hi, own_lo)
    copies[0].wait()
    eq = dot(embed, w_ref[0])
    copies[1].wait()
    ek = dot(embed, w_ref[1])
    copies[2].wait()
    ev = dot(embed, w_ref[2])
    copies[3].wait()
    gt = dot(head_t, w_ref[3])
    pair = 2 * embed.shape[0]
    for p in range(eq.shape[1] // pair):
        here = slice(p * pair, (p + 1) * pair)
        q, k, v, g = eq[:, here], ek[:, here], ev[:, here], gt[:, here]
        k2, v2, g2 = by_head(k), by_head(v), rows_cat(g, g)
        b = dot_nt(k2, rows_cat(q, q) * scale, HIGH)
        b_ref[here, :] = lanes_cat(*split(b))
        a = dot_nt(v2, g2, HIGH)
        hi, lo = split(a)
        at_ref[here, :] = jnp.where(left_half(a.shape), hi.astype(F32), lo.astype(F32)).astype(BF16)
        a = dot_nt(g2, v2, HIGH)
        hi, lo = split(a)
        ah_ref[:, here] = jnp.where(top_half(a.shape), hi.astype(F32), lo.astype(F32)).astype(BF16)
        diag_ref[0, :, here] = rows_cat(*split(by_head(q)))
        diag_ref[1, :, here] = rows_cat(*split(by_head(g)))
        cols_ref[0, :, here] = rows_cat(*split(k))
        cols_ref[1, :, here] = rows_cat(*split(v))


def forward_kernel(
    kept_ref, k1_ref, k2_ref, embed_ref, b_ref, ah_ref,
    e_ref, c_ref, inv_ref, part_ref, u_ref, ut_ref,
    q_ref, s0_ref, s1_ref,
):
    step = pl.program_id(0)
    last = pl.num_programs(0) - 1
    vox, rows = kept_ref.shape
    pair = 2 * vox
    dim = embed_ref.shape[1]

    def scores(head, s_ref):
        q = q_ref[pl.ds(pl.multiple_of(head * vox, vox), vox), :]
        s_ref[...] = dot(u_ref[:, :pair], rows_cat(q, q))

    @pl.when(step == 0)
    def _():
        embed_t = embed_ref[...].astype(F32).T.astype(BF16)
        for j, ref in enumerate((kept_ref, k1_ref, k2_ref)):
            kept = ref[...]
            hidden = dot(embed_t, kept)
            rms = lax.rsqrt(jnp.sum(hidden * hidden, 0, keepdims=True) / dim + 1e-06)
            u = kept.astype(F32) * rms
            hi, lo = split(u)
            here = slice(j * rows, (j + 1) * rows)
            both = rows_cat(hi, lo)
            ut_ref[:pair, here] = both
            ut_ref[pair:, here] = jnp.ones((ONES, rows), BF16)
            u_ref[here, :pair] = rows_cat(hi.astype(F32), lo.astype(F32)).T.astype(BF16)
            lane = lax.broadcasted_iota(jnp.int32, (rows, pair), 1)
            u_ref[here, pair:] = jnp.where(lane < 2, -1.0, 0.0).astype(BF16)
            if j == 0:
                q_ref[...] = dot(b_ref[...], rows_cat(both, both)).astype(BF16)
        scores(0, s0_ref)

    def softmax(i, s_ref):
        s = s_ref[...]
        e_ref[i] = jnp.exp2(s - jnp.max(s, 0, keepdims=True)).astype(BF16)

    def context(i):
        c = dot(ut_ref[...], e_ref[i])
        inv = 1.0 / c[pair : pair + 8]
        c = (c[:vox] + c[vox:pair]) * inv[:1]
        inv_ref[i] = inv
        here = pl.ds(pl.multiple_of((2 * step + i) * vox, vox), vox)
        c_ref[here, :] = c
        return c

    scores(2 * step + 1, s1_ref)
    softmax(0, s0_ref)
    scores(jnp.minimum(2 * step + 2, 2 * last + 1), s0_ref)
    c0 = context(0)
    softmax(1, s1_ref)
    c1 = context(1)
    hi, lo = split(rows_cat(c0, c1))
    ah = ah_ref[:, pl.ds(pl.multiple_of(step * pair, pair), pair)]
    p2 = dot(ah, hi)
    term = p2[:vox] + p2[vox:] + dot(ah[:vox], lo)

    @pl.when(step == 0)
    def _():
        part_ref[...] = term

    @pl.when(step > 0)
    def _():
        part_ref[...] += term


def backward_kernel(
    loss_weight, factor,
    part_ref, other_ref, vol_ref, mask_ref, kept_ref, own_ref, at_ref, c_ref, inv_ref, e_ref, u_ref, ut_ref,
    sums_ref,
    a_ref, gp_ref,
):
    step = pl.program_id(0)
    vox, rows = vol_ref.shape
    pair = 2 * vox

    @pl.when(step == 0)
    def _():
        kept = kept_ref[...]
        predicted = dot(own_ref[...], rows_cat(kept, kept)) + (part_ref[...] + other_ref[...])
        gp = mask_ref[...].astype(F32) * (predicted - vol_ref[...].astype(F32)) * loss_weight
        gp2 = rows_cat(gp, gp)
        gp_ref[...] = gp2.T.astype(BF16)
        a_ref[...] = dot(at_ref[...], gp2.astype(BF16)).astype(BF16)

    ms, ns = [], []
    row = lax.broadcasted_iota(jnp.int32, (pair, rows), 0)
    for i in range(2):
        here = pl.ds(pl.multiple_of((2 * step + i) * vox, vox), vox)
        a = a_ref[here, :]
        c = c_ref[here, :]
        off = jnp.sum(a.astype(F32) * c, 0, keepdims=True)
        off_hi = off.astype(BF16).astype(F32)
        tail = jnp.where(row == 0, off_hi, jnp.where(row == 1, off - off_hi, 0.0)).astype(BF16)
        t = dot(u_ref[...], rows_cat(a, a, tail))
        ds = (e_ref[i].astype(F32) * t).astype(BF16)
        x = dot(ut_ref[:pair, :], ds)
        x = (x[:vox] + x[vox:]) * (inv_ref[i, :1] * factor)
        m = dot(rows_cat(*split(x)), u_ref[:rows, :pair])
        m = m[:vox] + m[vox:]
        ms.append(m + pltpu.roll(m, vox, 1))
        n = dot(rows_cat(*split(c)), gp_ref[...])
        ns.append(n[:vox] + n[vox:])
    left = left_half((vox, pair))
    here = pl.ds(pl.multiple_of(step * pair, pair), pair)
    sums_ref[:vox, here] = jnp.where(left, ms[0], ms[1])
    sums_ref[vox:, here] = jnp.where(left, ns[0], ns[1])


def final_kernel(m_ref, n_ref, diag_ref, cols_ref, rows_ref, qkv_ref, out_ref):
    vox = m_ref.shape[0]
    pair = 2 * vox
    left = left_half((vox, pair))

    def row_form(x, e2):
        hi, lo = split(x)
        return dot(lanes_cat(hi, hi), e2) + dot(lo, e2[:pair])

    def col_form(x, e2):
        hi, lo = split(x.T)
        both = dot(lanes_cat(hi, hi), e2) + dot(lo, e2[:vox])
        return jnp.where(left, both[:vox], both[vox:])

    def put(j, t):
        return dot(rows_ref[j], rows_cat(*split(t)))

    for p in range(m_ref.shape[1] // pair):
        cols = slice(p * pair, (p + 1) * pair)
        m, n = m_ref[:, cols], n_ref[:, cols]
        qkv_ref[0, :, cols] = put(0, col_form(m, cols_ref[0, :, cols]))
        qkv_ref[1, :, cols] = put(0, row_form(m, diag_ref[0, :, cols]))
        qkv_ref[2, :, cols] = put(0, row_form(n, diag_ref[1, :, cols]))
        out_ref[:, cols] = put(1, col_form(n, cols_ref[1, :, cols]))


def shifted(x, axis, mask):
    return lax.ppermute(x, axis, [(i, i ^ mask) for i in range(lax.axis_size(axis))])


def sum_over(x, axis):
    half = x.shape[0] // 2
    odd = lax.axis_index(axis) % 2 == 1
    top, bottom = x[:half], x[half:]
    mine = jnp.where(odd, bottom, top) + shifted(jnp.where(odd, top, bottom), axis, 1)
    bits = [1 << b for b in range(1, lax.axis_size(axis).bit_length() - 1)]
    groups = [bits[:2]] + [[b] for b in bits[2:]]
    for group in groups:
        masks = [0]
        for b in group:
            masks += [m ^ b for m in masks]
        sent = mine.astype(BF16)
        parts = [mine] + [shifted(sent, axis, m).astype(F32) for m in masks[1:]]
        mine = functools.reduce(jnp.add, parts)
    other = shifted(mine, axis, 1)
    return jnp.where(odd, other, mine), jnp.where(odd, mine, other)


def struct(shape, dtype):
    return jax.ShapeDtypeStruct(shape, dtype)


def whole(shape):
    return pl.BlockSpec(shape, lambda *_: (0,) * len(shape))


def per_device(volume, vox_mask, embed, w_qkv, w_out, w_head):
    rows, vox = volume.shape
    dim, width = w_qkv.shape[1:]
    heads = width // vox
    pair = 2 * vox
    steps = heads // 2
    factor = (dim // HEADS) ** (-0.5)
    seq = lax.axis_size("seq")
    keys = (LEVELS + 1) * rows
    loss_weight = 256.0 / math.sqrt(rows * seq)

    vol_t, mask_t, head_t = volume.T, vox_mask.T, w_head.T
    kept = vol_t * (1 - mask_t).astype(BF16)
    others = [shifted(kept, "seq", 1 << bit) for bit in range(LEVELS)]

    hbm = pl.BlockSpec(memory_space=pltpu.MemorySpace.HBM)
    vmem = pl.BlockSpec(memory_space=pltpu.MemorySpace.VMEM)
    b, at, ah, diag, cols, own = pl.pallas_call(
        functools.partial(weights_kernel, factor * math.log2(math.e)),
        in_specs=[vmem, hbm, hbm, vmem],
        out_specs=[vmem] * 6,
        out_shape=(
            struct((width, 4 * vox), BF16),
            struct((width, pair), BF16),
            struct((pair, width), BF16),
            struct((2, 2 * pair, width), BF16),
            struct((2, pair, width), BF16),
            struct((vox, pair), BF16),
        ),
        scratch_shapes=[pltpu.VMEM((4, dim, width), BF16), pltpu.SemaphoreType.DMA((4,))],
        name="weights",
        compiler_params=pltpu.CompilerParams(vmem_limit_bytes=20 * MIB),
    )(embed, w_qkv, w_out, head_t)

    e, c, inv, part, u, ut = pl.pallas_call(
        forward_kernel,
        grid=(steps,),
        in_specs=[whole((vox, rows))] * 3 + [whole((vox, dim)), whole((width, 4 * vox)), whole((pair, width))],
        out_specs=(
            pl.BlockSpec((2, keys, rows), lambda i: (i, 0, 0)),
            whole((width, rows)),
            pl.BlockSpec((2, 8, rows), lambda i: (i, 0, 0)),
            whole((vox, rows)),
            whole((keys, 2 * pair)),
            whole((pair + ONES, keys)),
        ),
        out_shape=(
            struct((heads, keys, rows), BF16),
            struct((width, rows), F32),
            struct((heads, 8, rows), F32),
            struct((vox, rows), F32),
            struct((keys, 2 * pair), BF16),
            struct((pair + ONES, keys), BF16),
        ),
        scratch_shapes=[
            pltpu.VMEM((width, rows), BF16),
            pltpu.VMEM((keys, rows), F32),
            pltpu.VMEM((keys, rows), F32),
        ],
        name="forward",
        compiler_params=pltpu.CompilerParams(vmem_limit_bytes=40 * MIB),
    )(kept, *others, embed, b, ah)

    other = shifted(part, "head", 1)

    sums = pl.pallas_call(
        functools.partial(backward_kernel, loss_weight, factor),
        grid=(steps,),
        in_specs=[whole((vox, rows))] * 5
        + [
            whole((vox, pair)),
            whole((width, pair)),
            whole((width, rows)),
            pl.BlockSpec((2, 8, rows), lambda i: (i, 0, 0)),
            pl.BlockSpec((2, keys, rows), lambda i: (i, 0, 0)),
            whole((keys, 2 * pair)),
            whole((pair + ONES, keys)),
        ],
        out_specs=whole((pair, width)),
        out_shape=struct((pair, width), F32),
        scratch_shapes=[pltpu.VMEM((width, rows), BF16), pltpu.VMEM((rows, pair), BF16)],
        name="backward",
        compiler_params=pltpu.CompilerParams(vmem_limit_bytes=40 * MIB),
    )(part, other, vol_t, mask_t, kept, own, at, c, inv, e, u, ut)

    m, n = sum_over(sums, "seq")

    piece = dim // seq
    start = lax.axis_index("seq") * piece
    mine = [lax.dynamic_slice_in_dim(x, start, piece, 1).T for x in (embed, head_t)]
    mine = jnp.stack([jnp.concatenate([x, x], 1) for x in mine])
    return pl.pallas_call(
        final_kernel,
        out_shape=(struct((3, piece, width), F32), struct((piece, width), F32)),
        name="final",
    )(m, n, diag, cols, mine)


def solution(mesh):
    return jax.shard_map(
        per_device,
        mesh=mesh,
        in_specs=(P("seq", None), P("seq", None), P(), P(None, None, "head"), P(None, "head"), P()),
        out_specs=(P(None, "seq", "head"), P("seq", "head")),
        check_vma=False,
    )
```

```python
import functools
import math

import jax
import jax.numpy as jnp
from jax import lax
from jax.experimental import pallas as pl
from jax.experimental.pallas import tpu as pltpu
from jax.sharding import PartitionSpec as P

HEADS = 16
LEVELS = 2
F32 = jnp.float32
BF16 = jnp.bfloat16
ONES = 16
MIB = 1 << 20
FWD_MIB = 28
BWD_MIB = 28


def dot(a, b):
    return jnp.dot(a, b, preferred_element_type=F32)


def dot_nt(a, b):
    return lax.dot_general(a, b, (((1,), (1,)), ((), ())), preferred_element_type=F32)


def split(x):
    high = x.astype(BF16)
    return high, (x - high.astype(F32)).astype(BF16)


def rows_cat(*parts):
    return jnp.concatenate(parts, 0)


def lanes_cat(*parts):
    return jnp.concatenate(parts, 1)


def left_half(shape):
    return lax.broadcasted_iota(jnp.int32, shape, 1) < shape[1] // 2


def top_half(shape):
    return lax.broadcasted_iota(jnp.int32, shape, 0) < shape[0] // 2


def by_head(pair):
    left = left_half(pair.shape)
    return rows_cat(jnp.where(left, pair, 0.0), jnp.where(left, 0.0, pair))


def product(x, y):
    x_hi, x_lo = split(x)
    y_hi, y_lo = split(y)
    return dot_nt(lanes_cat(x_hi, x_lo), lanes_cat(y_hi, y_hi)) + dot_nt(x_hi, y_lo)


def weights_kernel(
    scale, seq_axis, piece, embed_hbm, head_t_hbm, w_qkv_hbm, w_out_hbm,
    b_ref, at_ref, ah_ref, terms_ref, own_ref, embed_t_ref, rows_ref,
    embed_ref, head_t_ref, w_ref, sem,
):
    small = [pltpu.make_async_copy(embed_hbm, embed_ref, sem.at[4])]
    small.append(pltpu.make_async_copy(head_t_hbm, head_t_ref, sem.at[5]))
    for copy in small:
        copy.start()
    copies = [pltpu.make_async_copy(w_qkv_hbm.at[j], w_ref.at[j], sem.at[j]) for j in range(3)]
    copies.append(pltpu.make_async_copy(w_out_hbm, w_ref.at[3], sem.at[3]))
    for copy in copies:
        copy.start()
    for copy in small:
        copy.wait()
    embed = embed_ref[...]
    head_t = head_t_ref[...]
    embed_t_ref[...] = embed.astype(F32).T.astype(BF16)
    own = dot_nt(head_t, embed)
    own_hi, own_lo = split(own)
    own_ref[...] = lanes_cat(own_hi, own_lo)
    first = lax.axis_index(seq_axis) * piece
    shape = (piece, embed.shape[1])
    wanted = lax.broadcasted_iota(jnp.int32, shape, 0) + first == lax.broadcasted_iota(jnp.int32, shape, 1)
    pick = jnp.where(wanted, 1.0, 0.0).astype(BF16)
    rows_ref[0] = dot_nt(pick, rows_cat(embed, embed)).astype(BF16)
    rows_ref[1] = dot_nt(pick, rows_cat(head_t, head_t)).astype(BF16)
    copies[0].wait()
    eq = dot(embed, w_ref[0])
    copies[1].wait()
    ek = dot(embed, w_ref[1])
    copies[2].wait()
    ev = dot(embed, w_ref[2])
    copies[3].wait()
    gt = dot(head_t, w_ref[3])
    pair = 2 * embed.shape[0]
    for p in range(eq.shape[1] // pair):
        here = slice(p * pair, (p + 1) * pair)
        q, k, v, g = eq[:, here], ek[:, here], ev[:, here], gt[:, here]
        k2, v2, g2 = by_head(k), by_head(v), rows_cat(g, g)
        b = product(k2, rows_cat(q, q) * scale)
        b_ref[here, :] = lanes_cat(*split(b))
        a = product(v2, g2)
        hi, lo = split(a)
        at_ref[here, :] = jnp.where(left_half(a.shape), hi.astype(F32), lo.astype(F32)).astype(BF16)
        a = product(g2, v2)
        hi, lo = split(a)
        ah_ref[:, here] = jnp.where(top_half(a.shape), hi.astype(F32), lo.astype(F32)).astype(BF16)
        for j, x in enumerate((q, k, v, g)):
            terms_ref[j, :, here] = rows_cat(*split(x))


def forward_kernel(
    kept_ref, k1_ref, k2_ref, embed_t_ref, b_ref, ah_ref, own_ref,
    e_ref, c_ref, inv_ref, part_ref, sent_ref, u_ref, ut_ref,
    q_ref, s0_ref, s1_ref, top_ref,
):
    step = pl.program_id(0)
    last = pl.num_programs(0) - 1
    vox, rows = kept_ref.shape
    pair = 2 * vox
    dim = embed_t_ref.shape[0]
    keys = u_ref.shape[0]
    chunk = min(256, rows)
    chunks = keys // chunk

    def queries(head):
        q = q_ref[pl.ds(pl.multiple_of(head * vox, vox), vox), :]
        return rows_cat(q, q)

    def scores(j, q, s_ref, top):
        here = slice(j * chunk, (j + 1) * chunk)
        s = dot(u_ref[here, :pair], q)
        s_ref[here, :] = s
        highest = jnp.max(s.reshape(chunk // 8, 8, rows), 0)
        return highest if top is None else jnp.maximum(top, highest)

    @pl.when(step == 0)
    def _():
        embed_t = embed_t_ref[...]
        for j, ref in enumerate((kept_ref, k1_ref, k2_ref)):
            kept = ref[...]
            hidden = dot(embed_t, kept)
            rms = lax.rsqrt(jnp.sum(hidden * hidden, 0, keepdims=True) / dim + 1e-06)
            u = kept.astype(F32) * rms
            hi, lo = split(u)
            here = slice(j * rows, (j + 1) * rows)
            both = rows_cat(hi, lo)
            ut_ref[:pair, here] = both
            ut_ref[pair:, here] = jnp.ones((ONES, rows), BF16)
            u_ref[here, :pair] = rows_cat(hi.astype(F32), lo.astype(F32)).T.astype(BF16)
            lane = lax.broadcasted_iota(jnp.int32, (rows, pair), 1)
            u_ref[here, pair:] = jnp.where(lane < 2, -1.0, 0.0).astype(BF16)
            if j == 0:
                q_ref[...] = dot(b_ref[...], rows_cat(both, both)).astype(BF16)
        top = None
        q = queries(0)
        for j in range(chunks):
            top = scores(j, q, s0_ref, top)
        top_ref[...] = top

    def head(i, s_ref, top, after, after_ref):
        top = jnp.max(top, 0, keepdims=True)
        q = queries(after)
        next_top, c = None, None
        for j in range(chunks):
            here = slice(j * chunk, (j + 1) * chunk)
            next_top = scores(j, q, after_ref, next_top)
            e = jnp.exp2(s_ref[here, :] - top).astype(BF16)
            e_ref[i, here, :] = e
            term = dot(ut_ref[:, here], e)
            c = term if c is None else c + term
        inv = 1.0 / c[pair : pair + 8]
        c = (c[:vox] + c[vox:pair]) * inv[:1]
        inv_ref[i] = inv
        here = pl.ds(pl.multiple_of((2 * step + i) * vox, vox), vox)
        c_ref[here, :] = c
        return c, next_top

    c0, top = head(0, s0_ref, top_ref[...], 2 * step + 1, s1_ref)
    c1, top = head(1, s1_ref, top, jnp.minimum(2 * step + 2, 2 * last + 1), s0_ref)
    top_ref[...] = top
    hi, lo = split(rows_cat(c0, c1))
    ah = ah_ref[:, pl.ds(pl.multiple_of(step * pair, pair), pair)]
    p2 = dot(ah, hi)
    term = p2[:vox] + p2[vox:] + dot(ah[:vox], lo)

    @pl.when(step == 0)
    def _():
        part_ref[...] = term

    @pl.when(step > 0)
    def _():
        part_ref[...] += term

    @pl.when(step == last)
    def _():
        kept = kept_ref[...]
        sent_ref[...] = part_ref[...].astype(BF16)
        part_ref[...] += dot(own_ref[...], rows_cat(kept, kept))


def backward_kernel(
    loss_weight, factor,
    part_ref, other_ref, held_ref, mask_ref, at_ref, c_ref, inv_ref, e_ref, u_ref, ut_ref,
    sums_ref,
    a_ref, gp_ref,
):
    step = pl.program_id(0)
    vox, rows = held_ref.shape
    pair = 2 * vox

    @pl.when(step == 0)
    def _():
        predicted = part_ref[...] + other_ref[...].astype(F32)
        gp = (mask_ref[...].astype(F32) * predicted - held_ref[...].astype(F32)) * loss_weight
        gp2 = rows_cat(gp, gp)
        gp_ref[...] = gp2.T.astype(BF16)
        a_ref[...] = dot(at_ref[...], gp2.astype(BF16)).astype(BF16)

    ms, ns = [], []
    row = lax.broadcasted_iota(jnp.int32, (pair, rows), 0)
    for i in range(2):
        here = pl.ds(pl.multiple_of((2 * step + i) * vox, vox), vox)
        a = a_ref[here, :]
        c = c_ref[here, :]
        off = jnp.sum(a.astype(F32) * c, 0, keepdims=True)
        off_hi = off.astype(BF16).astype(F32)
        tail = jnp.where(row == 0, off_hi, jnp.where(row == 1, off - off_hi, 0.0)).astype(BF16)
        t = dot(u_ref[...], rows_cat(a, a, tail))
        ds = (e_ref[i].astype(F32) * t).astype(BF16)
        x = dot(ut_ref[:pair, :], ds)
        x = (x[:vox] + x[vox:]) * (inv_ref[i, :1] * factor)
        m = dot(rows_cat(*split(x)), u_ref[:rows, :pair])
        m = m[:vox] + m[vox:]
        ms.append(m + pltpu.roll(m, vox, 1))
        n = dot(rows_cat(*split(c)), gp_ref[...])
        ns.append(n[:vox] + n[vox:])
    left = left_half((vox, pair))
    here = pl.ds(pl.multiple_of(step * pair, pair), pair)
    sums_ref[:vox, here] = jnp.where(left, ms[0], ms[1])
    sums_ref[vox:, here] = jnp.where(left, ns[0], ns[1])


def final_kernel(seq_axis, mine_ref, other_ref, terms_ref, rows_ref, qkv_ref, out_ref):
    vox = mine_ref.shape[0]
    odd = lax.axis_index(seq_axis) % 2 == 1
    pair = 2 * vox
    left = left_half((vox, pair))

    def row_form(x, e2):
        e2 = e2.astype(F32)
        e2 = rows_cat(by_head(e2[:vox]), by_head(e2[vox:])).astype(BF16)
        hi, lo = split(x)
        return dot(lanes_cat(hi, hi), e2) + dot(lo, e2[:pair])

    def col_form(x, e2):
        hi, lo = split(x.T)
        both = dot(lanes_cat(hi, hi), e2) + dot(lo, e2[:vox])
        return jnp.where(left, both[:vox], both[vox:])

    def put(j, t):
        return dot(rows_ref[j], rows_cat(*split(t)))

    for p in range(mine_ref.shape[1] // pair):
        cols = slice(p * pair, (p + 1) * pair)
        mine, other = mine_ref[:, cols], other_ref[:, cols]
        m, n = jnp.where(odd, other, mine), jnp.where(odd, mine, other)
        qkv_ref[0, :, cols] = put(0, col_form(m, terms_ref[1, :, cols]))
        qkv_ref[1, :, cols] = put(0, row_form(m, terms_ref[0, :, cols]))
        qkv_ref[2, :, cols] = put(0, row_form(n, terms_ref[3, :, cols]))
        out_ref[:, cols] = put(1, col_form(n, terms_ref[2, :, cols]))


def shifted(x, axis, mask):
    return lax.ppermute(x, axis, [(i, i ^ mask) for i in range(lax.axis_size(axis))])


def sum_over(x, axis):
    half = x.shape[0] // 2
    odd = lax.axis_index(axis) % 2 == 1
    top, bottom = x[:half], x[half:]
    mine = jnp.where(odd, bottom, top) + shifted(jnp.where(odd, top, bottom), axis, 1)
    bits = [1 << b for b in range(1, lax.axis_size(axis).bit_length() - 1)]
    groups = [bits[:2]] + [[b] for b in bits[2:]]
    for group in groups:
        masks = [0]
        for b in group:
            masks += [m ^ b for m in masks]
        sent = mine.astype(BF16)
        parts = [mine] + [shifted(sent, axis, m).astype(F32) for m in masks[1:]]
        mine = functools.reduce(jnp.add, parts)
    return mine, shifted(mine, axis, 1)


def in_hbm(x):
    return pltpu.with_memory_space_constraint(x, pltpu.MemorySpace.HBM)


def struct(shape, dtype):
    return jax.ShapeDtypeStruct(shape, dtype)


def whole(shape):
    return pl.BlockSpec(shape, lambda *_: (0,) * len(shape))


def per_device(volume, vox_mask, embed, w_qkv, w_out, w_head):
    rows, vox = volume.shape
    dim, width = w_qkv.shape[1:]
    heads = width // vox
    pair = 2 * vox
    steps = heads // 2
    factor = (dim // HEADS) ** (-0.5)
    seq = lax.axis_size("seq")
    keys = (LEVELS + 1) * rows
    loss_weight = 256.0 / math.sqrt(rows * seq)

    vol_t, mask_t, head_t = volume.T, vox_mask.T, w_head.T
    mask = mask_t.astype(BF16)
    kept, held, mask = lax.optimization_barrier((vol_t * (1 - mask_t).astype(BF16), vol_t * mask, mask))
    others = [shifted(kept, "seq", 1 << bit) for bit in range(LEVELS)]
    piece = dim // seq

    hbm = pl.BlockSpec(memory_space=pltpu.MemorySpace.HBM)
    vmem = pl.BlockSpec(memory_space=pltpu.MemorySpace.VMEM)
    b, at, ah, terms, own, embed_t, picked = pl.pallas_call(
        functools.partial(weights_kernel, factor * math.log2(math.e), "seq", piece),
        in_specs=[hbm] * 4,
        out_specs=[vmem] * 7,
        out_shape=(
            struct((width, 4 * vox), BF16),
            struct((width, pair), BF16),
            struct((pair, width), BF16),
            struct((4, pair, width), BF16),
            struct((vox, pair), BF16),
            struct((dim, vox), BF16),
            struct((2, piece, pair), BF16),
        ),
        scratch_shapes=[
            pltpu.VMEM((vox, dim), BF16),
            pltpu.VMEM((vox, dim), BF16),
            pltpu.VMEM((4, dim, width), BF16),
            pltpu.SemaphoreType.DMA((6,)),
        ],
        name="weights",
        compiler_params=pltpu.CompilerParams(vmem_limit_bytes=24 * MIB),
    )(in_hbm(embed), in_hbm(head_t), in_hbm(w_qkv), in_hbm(w_out))

    e, c, inv, part, sent, u, ut = pl.pallas_call(
        forward_kernel,
        grid=(steps,),
        in_specs=[whole((vox, rows))] * 3 + [whole((dim, vox)), whole((width, 4 * vox)), whole((pair, width))]
        + [whole((vox, pair))],
        out_specs=(
            pl.BlockSpec((2, keys, rows), lambda i: (i, 0, 0)),
            whole((width, rows)),
            pl.BlockSpec((2, 8, rows), lambda i: (i, 0, 0)),
            whole((vox, rows)),
            whole((vox, rows)),
            whole((keys, 2 * pair)),
            whole((pair + ONES, keys)),
        ),
        out_shape=(
            pltpu.MemorySpace.HBM((heads, keys, rows), BF16),
            struct((width, rows), F32),
            struct((heads, 8, rows), F32),
            struct((vox, rows), F32),
            struct((vox, rows), BF16),
            struct((keys, 2 * pair), BF16),
            struct((pair + ONES, keys), BF16),
        ),
        scratch_shapes=[
            pltpu.VMEM((width, rows), BF16),
            pltpu.VMEM((keys, rows), F32),
            pltpu.VMEM((keys, rows), F32),
            pltpu.VMEM((8, rows), F32),
        ],
        name="forward",
        compiler_params=pltpu.CompilerParams(vmem_limit_bytes=FWD_MIB * MIB),
    )(kept, *others, embed_t, b, ah, own)

    other = shifted(sent, "head", 1)

    sums = pl.pallas_call(
        functools.partial(backward_kernel, loss_weight, factor),
        grid=(steps,),
        in_specs=[whole((vox, rows))] * 4
        + [
            whole((width, pair)),
            whole((width, rows)),
            pl.BlockSpec((2, 8, rows), lambda i: (i, 0, 0)),
            pl.BlockSpec((2, keys, rows), lambda i: (i, 0, 0)),
            whole((keys, 2 * pair)),
            whole((pair + ONES, keys)),
        ],
        out_specs=whole((pair, width)),
        out_shape=struct((pair, width), F32),
        scratch_shapes=[pltpu.VMEM((width, rows), BF16), pltpu.VMEM((rows, pair), BF16)],
        name="backward",
        compiler_params=pltpu.CompilerParams(vmem_limit_bytes=BWD_MIB * MIB),
    )(part, other, held, mask, at, c, inv, in_hbm(e), u, ut)

    mine, swapped = sum_over(sums, "seq")
    return pl.pallas_call(
        functools.partial(final_kernel, "seq"),
        out_shape=(struct((3, piece, width), F32), struct((piece, width), F32)),
        name="final",
        compiler_params=pltpu.CompilerParams(vmem_limit_bytes=8 * MIB),
    )(mine, swapped, terms, picked)


def solution(mesh):
    return jax.shard_map(
        per_device,
        mesh=mesh,
        in_specs=(P("seq", None), P("seq", None), P(), P(None, None, "head"), P(None, "head"), P()),
        out_specs=(P(None, "seq", "head"), P("seq", "head")),
        check_vma=False,
    )
```

```python
import functools
import math

import jax
import jax.numpy as jnp
from jax import lax
from jax.experimental import pallas as pl
from jax.experimental.pallas import tpu as pltpu
from jax.sharding import PartitionSpec as P

HEADS = 16
LEVELS = 2
F32 = jnp.float32
BF16 = jnp.bfloat16
ONES = 16
MIB = 1 << 20
FWD_MIB = 34
BWD_MIB = 34


def dot(a, b):
    return jnp.dot(a, b, preferred_element_type=F32)


def dot_nt(a, b):
    return lax.dot_general(a, b, (((1,), (1,)), ((), ())), preferred_element_type=F32)


def split(x):
    high = x.astype(BF16)
    return high, (x - high.astype(F32)).astype(BF16)


def rows_cat(*parts):
    return jnp.concatenate(parts, 0)


def lanes_cat(*parts):
    return jnp.concatenate(parts, 1)


def left_half(shape):
    return lax.broadcasted_iota(jnp.int32, shape, 1) < shape[1] // 2


def top_half(shape):
    return lax.broadcasted_iota(jnp.int32, shape, 0) < shape[0] // 2


def by_head(pair):
    left = left_half(pair.shape)
    return rows_cat(jnp.where(left, pair, 0.0), jnp.where(left, 0.0, pair))


def product(x, y):
    x_hi, x_lo = split(x)
    y_hi, y_lo = split(y)
    return dot_nt(lanes_cat(x_hi, x_lo), lanes_cat(y_hi, y_hi)) + dot_nt(x_hi, y_lo)


def unit_rows(kept, embed_t):
    hidden = dot(embed_t, kept)
    rms = lax.rsqrt(jnp.sum(hidden * hidden, 0, keepdims=True) / embed_t.shape[0] + 1e-06)
    hi, lo = split(kept.astype(F32) * rms)
    return rows_cat(hi, lo), rows_cat(hi.astype(F32), lo.astype(F32)).T.astype(BF16)


def weights_kernel(
    scale, seq_axis, piece, kept_ref, embed_hbm, head_t_hbm, w_qkv_hbm, w_out_hbm,
    q_ref, ut_ref, u_ref, at_ref, ah_ref, terms_ref, own_ref, embed_t_ref, rows_ref,
    embed_ref, head_t_ref, w_ref, sem,
):
    small = [pltpu.make_async_copy(embed_hbm, embed_ref, sem.at[4])]
    small.append(pltpu.make_async_copy(head_t_hbm, head_t_ref, sem.at[5]))
    for copy in small:
        copy.start()
    copies = [pltpu.make_async_copy(w_qkv_hbm.at[j], w_ref.at[j], sem.at[j]) for j in range(3)]
    copies.append(pltpu.make_async_copy(w_out_hbm, w_ref.at[3], sem.at[3]))
    for copy in copies:
        copy.start()
    for copy in small:
        copy.wait()
    embed = embed_ref[...]
    head_t = head_t_ref[...]
    embed_t = embed.astype(F32).T.astype(BF16)
    embed_t_ref[...] = embed_t
    both, u_ref[...] = unit_rows(kept_ref[...], embed_t)
    ut_ref[...] = both
    own = dot_nt(head_t, embed)
    own_hi, own_lo = split(own)
    own_ref[...] = lanes_cat(own_hi, own_lo)
    first = lax.axis_index(seq_axis) * piece
    shape = (piece, embed.shape[1])
    wanted = lax.broadcasted_iota(jnp.int32, shape, 0) + first == lax.broadcasted_iota(jnp.int32, shape, 1)
    pick = jnp.where(wanted, 1.0, 0.0).astype(BF16)
    rows_ref[0] = dot_nt(pick, rows_cat(embed, embed)).astype(BF16)
    rows_ref[1] = dot_nt(pick, rows_cat(head_t, head_t)).astype(BF16)
    pair = 2 * embed.shape[0]
    copies[0].wait()
    eq = dot(embed, w_ref[0])
    copies[1].wait()
    ek = dot(embed, w_ref[1])
    pairs = [slice(p * pair, (p + 1) * pair) for p in range(eq.shape[1] // pair)]
    for here in pairs:
        q, k = eq[:, here], ek[:, here]
        b = product(by_head(k), rows_cat(q, q) * scale)
        q_ref[here, :] = dot(lanes_cat(*split(b)), rows_cat(both, both)).astype(BF16)
        terms_ref[0, :, here] = rows_cat(*split(q))
        terms_ref[1, :, here] = rows_cat(*split(k))
    copies[2].wait()
    ev = dot(embed, w_ref[2])
    copies[3].wait()
    gt = dot(head_t, w_ref[3])
    for here in pairs:
        v, g = ev[:, here], gt[:, here]
        v2, g2 = by_head(v), rows_cat(g, g)
        a = product(v2, g2)
        hi, lo = split(a)
        at_ref[here, :] = jnp.where(left_half(a.shape), hi.astype(F32), lo.astype(F32)).astype(BF16)
        a = product(g2, v2)
        hi, lo = split(a)
        ah_ref[:, here] = jnp.where(top_half(a.shape), hi.astype(F32), lo.astype(F32)).astype(BF16)
        terms_ref[2, :, here] = rows_cat(*split(v))
        terms_ref[3, :, here] = rows_cat(*split(g))


def forward_kernel(
    kept_ref, ut0_ref, u0_ref, k1_ref, k2_ref, embed_t_ref, q_ref, ah_ref, own_ref,
    e_hbm, c_ref, inv_ref, part_ref, sent_ref, u_ref, ut_ref,
    s0_ref, s1_ref, top_ref, e_ref, sem,
):
    vox, rows = kept_ref.shape
    heads, keys = e_ref.shape[:2]
    pair = 2 * vox
    chunk = min(256, rows)
    chunks = [slice(j * chunk, (j + 1) * chunk) for j in range(keys // chunk)]

    def stored(head):
        return pltpu.make_async_copy(e_ref.at[head], e_hbm.at[head], sem.at[head])

    embed_t = embed_t_ref[...]
    lane = lax.broadcasted_iota(jnp.int32, (rows, pair), 1)
    blocks = [(ut0_ref[...], u0_ref[...])] + [unit_rows(ref[...], embed_t) for ref in (k1_ref, k2_ref)]
    for j, (both, turned) in enumerate(blocks):
        here = slice(j * rows, (j + 1) * rows)
        ut_ref[:pair, here] = both
        ut_ref[pair:, here] = jnp.ones((ONES, rows), BF16)
        u_ref[here, :pair] = turned
        u_ref[here, pair:] = jnp.where(lane < 2, -1.0, 0.0).astype(BF16)

    def scores(head, s_ref):
        q = q_ref[pl.ds(pl.multiple_of(head * vox, vox), vox), :]
        q = rows_cat(q, q)
        top = None
        for here in chunks:
            s = dot(u_ref[here, :pair], q)
            s_ref[here, :] = s
            highest = jnp.max(s.reshape(chunk // 8, 8, rows), 0)
            top = highest if top is None else jnp.maximum(top, highest)
        return top

    def softmax(head, s_ref, top):
        top = jnp.max(top, 0, keepdims=True)
        for here in chunks:
            e_ref[head, here, :] = jnp.exp2(s_ref[here, :] - top).astype(BF16)
        c = dot(ut_ref[...], e_ref[head])
        inv = 1.0 / c[pair : pair + 8]
        inv_ref[head] = inv
        c_ref[pl.ds(pl.multiple_of(head * vox, vox), vox), :] = (c[:vox] + c[vox:pair]) * inv[:1]

    top_ref[...] = scores(0, s0_ref)

    def both_of(head, now_ref, next_ref):
        top = top_ref[...]
        top_ref[...] = scores(head + 1, next_ref)
        softmax(head, now_ref, top)

    @pl.loop(0, heads - 1)
    def _(head):
        @pl.when(head % 2 == 0)
        def _():
            both_of(head, s0_ref, s1_ref)

        @pl.when(head % 2 == 1)
        def _():
            both_of(head, s1_ref, s0_ref)

        stored(head).start()

    softmax(heads - 1, s1_ref if heads % 2 == 0 else s0_ref, top_ref[...])
    stored(heads - 1).start()
    hi, lo = split(c_ref[...])
    ah = ah_ref[...]
    p2 = dot(ah, hi)
    part = p2[:vox] + p2[vox:] + dot(ah[:vox], lo)
    sent_ref[...] = part.astype(BF16)
    kept = kept_ref[...]
    part_ref[...] = part + dot(own_ref[...], rows_cat(kept, kept))
    for head in range(heads):
        stored(head).wait()


def backward_kernel(
    loss_weight, factor,
    part_ref, other_ref, held_ref, mask_ref, at_ref, c_ref, inv_ref, e_hbm, u_ref, ut_ref,
    sums_ref,
    a_ref, e_ref, sem,
):
    vox, rows = held_ref.shape
    heads = e_ref.shape[0]
    pair = 2 * vox
    left = left_half((vox, pair))

    def loaded(head):
        return pltpu.make_async_copy(e_hbm.at[head], e_ref.at[head], sem.at[head])

    loaded(0).start()
    loaded(1).start()
    predicted = part_ref[...] + other_ref[...].astype(F32)
    gp = (mask_ref[...].astype(F32) * predicted - held_ref[...].astype(F32)) * loss_weight
    gp2 = rows_cat(gp, gp)
    turned = gp2.T.astype(BF16)
    a_ref[...] = dot(at_ref[...], gp2.astype(BF16)).astype(BF16)
    hi, lo = split(c_ref[...])
    n = dot(hi, turned) + dot(lo, turned)
    for p in range(n.shape[0] // pair):
        even, odd = n[p * pair : p * pair + vox], n[p * pair + vox : (p + 1) * pair]
        sums_ref[vox:, p * pair : (p + 1) * pair] = jnp.where(left, even, odd)
    row = lax.broadcasted_iota(jnp.int32, (pair, rows), 0)

    @pl.loop(0, heads // 2)
    def _(step):
        @pl.when(step < heads // 2 - 1)
        def _():
            loaded(2 * step + 2).start()
            loaded(2 * step + 3).start()

        loaded(2 * step).wait()
        loaded(2 * step + 1).wait()
        ms = []
        for i in range(2):
            here = pl.ds(pl.multiple_of((2 * step + i) * vox, vox), vox)
            a = a_ref[here, :]
            c = c_ref[here, :]
            off = jnp.sum(a.astype(F32) * c, 0, keepdims=True)
            off_hi = off.astype(BF16).astype(F32)
            tail = jnp.where(row == 0, off_hi, jnp.where(row == 1, off - off_hi, 0.0)).astype(BF16)
            t = dot(u_ref[...], rows_cat(a, a, tail))
            ds = (e_ref[2 * step + i].astype(F32) * t).astype(BF16)
            x = dot(ut_ref[:pair, :], ds)
            x = (x[:vox] + x[vox:]) * (inv_ref[2 * step + i, :1] * factor)
            m = dot(rows_cat(*split(x)), u_ref[:rows, :pair])
            m = m[:vox] + m[vox:]
            ms.append(m + pltpu.roll(m, vox, 1))
        here = pl.ds(pl.multiple_of(step * pair, pair), pair)
        sums_ref[:vox, here] = jnp.where(left, ms[0], ms[1])


def final_kernel(seq_axis, mine_ref, other_ref, terms_ref, rows_ref, qkv_ref, out_ref):
    vox = mine_ref.shape[0]
    odd = lax.axis_index(seq_axis) % 2 == 1
    pair = 2 * vox
    left = left_half((vox, pair))

    def row_form(x, e2):
        e2 = e2.astype(F32)
        e_hi, e_lo = by_head(e2[:vox]).astype(BF16), by_head(e2[vox:]).astype(BF16)
        hi, lo = split(x)
        return dot(lanes_cat(hi, lo, hi), rows_cat(e_hi, e_hi, e_lo))

    def col_form(x, e2):
        turned = rows_cat(x, x).T
        hi = turned.astype(BF16).astype(F32)
        parts = jnp.where(left_half(turned.shape), hi, turned - hi).astype(BF16)
        e_hi, e_lo = e2[:vox], e2[vox:]
        both = dot(lanes_cat(parts, parts), rows_cat(e_hi, e_hi, e_lo, e_lo))
        return jnp.where(left, both[:vox], both[vox:])

    terms = [[], [], [], []]
    for p in range(mine_ref.shape[1] // pair):
        cols = slice(p * pair, (p + 1) * pair)
        mine, other = mine_ref[:, cols], other_ref[:, cols]
        m, n = jnp.where(odd, other, mine), jnp.where(odd, mine, other)
        terms[0].append(col_form(m, terms_ref[1, :, cols]))
        terms[1].append(row_form(m, terms_ref[0, :, cols]))
        terms[2].append(row_form(n, terms_ref[3, :, cols]))
        terms[3].append(col_form(n, terms_ref[2, :, cols]))
    for j in range(3):
        qkv_ref[j] = dot(rows_ref[0], rows_cat(*split(lanes_cat(*terms[j]))))
    out_ref[...] = dot(rows_ref[1], rows_cat(*split(lanes_cat(*terms[3]))))


def shifted(x, axis, mask):
    return lax.ppermute(x, axis, [(i, i ^ mask) for i in range(lax.axis_size(axis))])


def sum_over(x, axis):
    half = x.shape[0] // 2
    odd = lax.axis_index(axis) % 2 == 1
    top, bottom = x[:half], x[half:]
    mine = jnp.where(odd, bottom, top) + shifted(jnp.where(odd, top, bottom), axis, 1)
    bits = [1 << b for b in range(1, lax.axis_size(axis).bit_length() - 1)]
    groups = [bits[:2]] + [[b] for b in bits[2:]]
    for group in groups:
        masks = [0]
        for b in group:
            masks += [m ^ b for m in masks]
        sent = mine.astype(BF16)
        parts = [mine] + [shifted(sent, axis, m).astype(F32) for m in masks[1:]]
        mine = functools.reduce(jnp.add, parts)
    return mine, shifted(mine, axis, 1)


def in_hbm(x):
    return pltpu.with_memory_space_constraint(x, pltpu.MemorySpace.HBM)


def struct(shape, dtype):
    return jax.ShapeDtypeStruct(shape, dtype)


def per_device(volume, vox_mask, embed, w_qkv, w_out, w_head):
    rows, vox = volume.shape
    dim, width = w_qkv.shape[1:]
    heads = width // vox
    pair = 2 * vox
    factor = (dim // HEADS) ** (-0.5)
    seq = lax.axis_size("seq")
    keys = (LEVELS + 1) * rows
    loss_weight = 256.0 / math.sqrt(rows * seq)

    vol_t, mask_t, head_t = volume.T, vox_mask.T, w_head.T
    mask = mask_t.astype(BF16)
    kept, held, mask = lax.optimization_barrier((vol_t * (1 - mask_t).astype(BF16), vol_t * mask, mask))
    others = [shifted(kept, "seq", 1 << bit) for bit in range(LEVELS)]
    piece = dim // seq

    hbm = pl.BlockSpec(memory_space=pltpu.MemorySpace.HBM)
    vmem = pl.BlockSpec(memory_space=pltpu.MemorySpace.VMEM)
    q, ut0, u0, at, ah, terms, own, embed_t, picked = pl.pallas_call(
        functools.partial(weights_kernel, factor * math.log2(math.e), "seq", piece),
        in_specs=[vmem] + [hbm] * 4,
        out_specs=[vmem] * 9,
        out_shape=(
            struct((width, rows), BF16),
            struct((pair, rows), BF16),
            struct((rows, pair), BF16),
            struct((width, pair), BF16),
            struct((pair, width), BF16),
            struct((4, pair, width), BF16),
            struct((vox, pair), BF16),
            struct((dim, vox), BF16),
            struct((2, piece, pair), BF16),
        ),
        scratch_shapes=[
            pltpu.VMEM((vox, dim), BF16),
            pltpu.VMEM((vox, dim), BF16),
            pltpu.VMEM((4, dim, width), BF16),
            pltpu.SemaphoreType.DMA((6,)),
        ],
        name="weights",
        compiler_params=pltpu.CompilerParams(vmem_limit_bytes=24 * MIB),
    )(kept, in_hbm(embed), in_hbm(head_t), in_hbm(w_qkv), in_hbm(w_out))

    e, c, inv, part, sent, u, ut = pl.pallas_call(
        forward_kernel,
        in_specs=[vmem] * 9,
        out_specs=(hbm,) + (vmem,) * 6,
        out_shape=(
            pltpu.MemorySpace.HBM((heads, keys, rows), BF16),
            struct((width, rows), F32),
            struct((heads, 8, rows), F32),
            struct((vox, rows), F32),
            struct((vox, rows), BF16),
            struct((keys, 2 * pair), BF16),
            struct((pair + ONES, keys), BF16),
        ),
        scratch_shapes=[
            pltpu.VMEM((keys, rows), F32),
            pltpu.VMEM((keys, rows), F32),
            pltpu.VMEM((8, rows), F32),
            pltpu.VMEM((heads, keys, rows), BF16),
            pltpu.SemaphoreType.DMA((heads,)),
        ],
        name="forward",
        compiler_params=pltpu.CompilerParams(vmem_limit_bytes=FWD_MIB * MIB),
    )(kept, ut0, u0, *others, embed_t, q, ah, own)

    other = shifted(sent, "head", 1)

    sums = pl.pallas_call(
        functools.partial(backward_kernel, loss_weight, factor),
        in_specs=[vmem] * 7 + [hbm] + [vmem] * 2,
        out_specs=vmem,
        out_shape=struct((pair, width), F32),
        scratch_shapes=[
            pltpu.VMEM((width, rows), BF16),
            pltpu.VMEM((heads, keys, rows), BF16),
            pltpu.SemaphoreType.DMA((heads,)),
        ],
        name="backward",
        compiler_params=pltpu.CompilerParams(vmem_limit_bytes=BWD_MIB * MIB),
    )(part, other, held, mask, at, c, inv, in_hbm(e), u, ut)

    mine, swapped = sum_over(sums, "seq")
    return pl.pallas_call(
        functools.partial(final_kernel, "seq"),
        out_shape=(struct((3, piece, width), F32), struct((piece, width), F32)),
        name="final",
        compiler_params=pltpu.CompilerParams(vmem_limit_bytes=8 * MIB),
    )(mine, swapped, terms, picked)


def solution(mesh):
    return jax.shard_map(
        per_device,
        mesh=mesh,
        in_specs=(P("seq", None), P("seq", None), P(), P(None, None, "head"), P(None, "head"), P()),
        out_specs=(P(None, "seq", "head"), P("seq", "head")),
        check_vma=False,
    )
```

```python
import functools
import math

import jax
import jax.numpy as jnp
from jax import lax
from jax.experimental import pallas as pl
from jax.experimental.pallas import tpu as pltpu
from jax.sharding import PartitionSpec as P

HEADS = 16
LEVELS = 2
F32 = jnp.float32
BF16 = jnp.bfloat16
ONES = 16
MIB = 1 << 20
FWD_MIB = 34
BWD_MIB = 34


def dot(a, b):
    return jnp.dot(a, b, preferred_element_type=F32)


def dot_nt(a, b):
    return lax.dot_general(a, b, (((1,), (1,)), ((), ())), preferred_element_type=F32)


def split(x):
    high = x.astype(BF16)
    return high, (x - high.astype(F32)).astype(BF16)


def rows_cat(*parts):
    return jnp.concatenate(parts, 0)


def lanes_cat(*parts):
    return jnp.concatenate(parts, 1)


def left_half(shape):
    return lax.broadcasted_iota(jnp.int32, shape, 1) < shape[1] // 2


def top_half(shape):
    return lax.broadcasted_iota(jnp.int32, shape, 0) < shape[0] // 2


def by_head(pair):
    left = left_half(pair.shape)
    return rows_cat(jnp.where(left, pair, 0.0), jnp.where(left, 0.0, pair))


def product(x, y):
    x_hi, x_lo = split(x)
    y_hi, y_lo = split(y)
    return dot_nt(lanes_cat(x_hi, x_lo), lanes_cat(y_hi, y_hi)) + dot_nt(x_hi, y_lo)


def unit_rows(kept, embed_t):
    hidden = dot(embed_t, kept)
    rms = lax.rsqrt(jnp.sum(hidden * hidden, 0, keepdims=True) / embed_t.shape[0] + 1e-06)
    hi, lo = split(kept.astype(F32) * rms)
    return rows_cat(hi, lo), rows_cat(hi.astype(F32), lo.astype(F32)).T.astype(BF16)


def weights_kernel(
    scale, kept_ref, embed_hbm, head_t_hbm, w_qkv_hbm, w_out_hbm,
    q_ref, ut_ref, u_ref, ah_ref, terms_ref, own_ref, embed_t_ref,
    embed_ref, head_t_ref, w_ref, sem,
):
    small = [pltpu.make_async_copy(embed_hbm, embed_ref, sem.at[4])]
    small.append(pltpu.make_async_copy(head_t_hbm, head_t_ref, sem.at[5]))
    for copy in small:
        copy.start()
    copies = [pltpu.make_async_copy(w_qkv_hbm.at[j], w_ref.at[j], sem.at[j]) for j in range(3)]
    copies.append(pltpu.make_async_copy(w_out_hbm, w_ref.at[3], sem.at[3]))
    for copy in copies:
        copy.start()
    for copy in small:
        copy.wait()
    embed = embed_ref[...]
    head_t = head_t_ref[...]
    embed_t = embed.astype(F32).T.astype(BF16)
    embed_t_ref[...] = embed_t
    both, u_ref[...] = unit_rows(kept_ref[...], embed_t)
    ut_ref[...] = both
    own = dot_nt(head_t, embed)
    own_hi, own_lo = split(own)
    own_ref[...] = lanes_cat(own_hi, own_lo)
    pair = 2 * embed.shape[0]
    copies[0].wait()
    eq = dot(embed, w_ref[0])
    copies[1].wait()
    ek = dot(embed, w_ref[1])
    pairs = [slice(p * pair, (p + 1) * pair) for p in range(eq.shape[1] // pair)]
    for here in pairs:
        q, k = eq[:, here], ek[:, here]
        b = product(by_head(k), rows_cat(q, q) * scale)
        q_ref[here, :] = dot(lanes_cat(*split(b)), rows_cat(both, both)).astype(BF16)
        terms_ref[0, :, here] = rows_cat(*split(q))
        terms_ref[1, :, here] = rows_cat(*split(k))
    copies[2].wait()
    ev = dot(embed, w_ref[2])
    copies[3].wait()
    gt = dot(head_t, w_ref[3])
    for here in pairs:
        v, g = ev[:, here], gt[:, here]
        v2, g2 = by_head(v), rows_cat(g, g)
        a = product(g2, v2)
        hi, lo = split(a)
        ah_ref[:, here] = jnp.where(top_half(a.shape), hi.astype(F32), lo.astype(F32)).astype(BF16)
        terms_ref[2, :, here] = rows_cat(*split(v))
        terms_ref[3, :, here] = rows_cat(*split(g))


def late_kernel(seq_axis, piece, after_ref, terms_ref, embed_hbm, head_t_hbm, at_ref, rows_ref, embed_ref, head_t_ref, sem):
    copies = [pltpu.make_async_copy(embed_hbm, embed_ref, sem.at[0])]
    copies.append(pltpu.make_async_copy(head_t_hbm, head_t_ref, sem.at[1]))
    for copy in copies:
        copy.start()
    vox = embed_ref.shape[0]
    pair = 2 * vox
    for p in range(terms_ref.shape[2] // pair):
        here = slice(p * pair, (p + 1) * pair)
        v, g = terms_ref[2, :, here].astype(F32), terms_ref[3, :, here]
        v_hi, v_lo = by_head(v[:vox]).astype(BF16), by_head(v[vox:]).astype(BF16)
        g_hi, g_lo = rows_cat(g[:vox], g[:vox]), rows_cat(g[vox:], g[vox:])
        a = dot_nt(lanes_cat(v_hi, v_lo), lanes_cat(g_hi, g_hi)) + dot_nt(v_hi, g_lo)
        hi = a.astype(BF16).astype(F32)
        at_ref[here, :] = jnp.where(left_half(a.shape), hi, a - hi).astype(BF16)
    for copy in copies:
        copy.wait()
    first = lax.axis_index(seq_axis) * piece
    shape = (piece, embed_ref.shape[1])
    wanted = lax.broadcasted_iota(jnp.int32, shape, 0) + first == lax.broadcasted_iota(jnp.int32, shape, 1)
    pick = jnp.where(wanted, 1.0, 0.0).astype(BF16)
    for j, ref in enumerate((embed_ref, head_t_ref)):
        rows_ref[j] = dot_nt(pick, rows_cat(ref[...], ref[...])).astype(BF16)


def forward_kernel(
    kept_ref, ut0_ref, u0_ref, k1_ref, k2_ref, embed_t_ref, q_ref, ah_ref, own_ref,
    e_hbm, c_ref, inv_ref, part_ref, sent_ref, u_ref, ut_ref,
    s0_ref, s1_ref, top_ref, e_ref, sem, last_sem,
):
    vox, rows = kept_ref.shape
    heads, keys = e_ref.shape[:2]
    pair = 2 * vox
    chunk = min(256, rows)
    chunks = [slice(j * chunk, (j + 1) * chunk) for j in range(keys // chunk)]

    def stored(head):
        return pltpu.make_async_copy(e_ref.at[head], e_hbm.at[head], sem.at[head])

    def piece(j):
        here = (heads - 1, pl.ds(j * chunk, chunk))
        return pltpu.make_async_copy(e_ref.at[here], e_hbm.at[here], last_sem.at[j])

    embed_t = embed_t_ref[...]
    blocks = [(ut0_ref[...], u0_ref[...])] + [unit_rows(ref[...], embed_t) for ref in (k1_ref, k2_ref)]
    for j, (both, turned) in enumerate(blocks):
        here = slice(j * rows, (j + 1) * rows)
        ut_ref[:pair, here] = both
        ut_ref[pair:, here] = jnp.ones((ONES, rows), BF16)
        u_ref[here, :] = turned

    def scores(head, s_ref):
        q = q_ref[pl.ds(pl.multiple_of(head * vox, vox), vox), :]
        q = rows_cat(q, q)
        top = None
        for here in chunks:
            s = dot(u_ref[here, :], q)
            s_ref[here, :] = s
            highest = jnp.max(s.reshape(chunk // 8, 8, rows), 0)
            top = highest if top is None else jnp.maximum(top, highest)
        return top

    def softmax(head, s_ref, top, leave=False):
        top = jnp.max(top, 0, keepdims=True)
        for j, here in enumerate(chunks):
            e_ref[head, here, :] = jnp.exp2(s_ref[here, :] - top).astype(BF16)
            if leave:
                piece(j).start()
        c = dot(ut_ref[...], e_ref[head])
        inv = 1.0 / c[pair : pair + 8]
        inv_ref[head] = inv
        c_ref[pl.ds(pl.multiple_of(head * vox, vox), vox), :] = (c[:vox] + c[vox:pair]) * inv[:1]

    top_ref[...] = scores(0, s0_ref)

    def both_of(head, now_ref, next_ref):
        top = top_ref[...]
        top_ref[...] = scores(head + 1, next_ref)
        softmax(head, now_ref, top)

    @pl.loop(0, heads - 1)
    def _(head):
        @pl.when(head % 2 == 0)
        def _():
            both_of(head, s0_ref, s1_ref)

        @pl.when(head % 2 == 1)
        def _():
            both_of(head, s1_ref, s0_ref)

        stored(head).start()

    softmax(heads - 1, s1_ref if heads % 2 == 0 else s0_ref, top_ref[...], True)
    hi, lo = split(c_ref[...])
    ah = ah_ref[...]
    p2 = dot(ah, hi)
    part = p2[:vox] + p2[vox:] + dot(ah[:vox], lo)
    sent_ref[...] = part.astype(BF16)
    kept = kept_ref[...]
    part_ref[...] = part + dot(own_ref[...], rows_cat(kept, kept))
    for head in range(heads - 1):
        stored(head).wait()
    for j in range(len(chunks)):
        piece(j).wait()


def backward_kernel(
    loss_weight, factor,
    part_ref, other_ref, held_ref, mask_ref, at_ref, c_ref, inv_ref, e_hbm, u_ref, ut_ref,
    sums_ref,
    a_ref, e_ref, sem,
):
    vox, rows = held_ref.shape
    heads = e_ref.shape[0]
    pair = 2 * vox
    left = left_half((vox, pair))

    def loaded(head):
        return pltpu.make_async_copy(e_hbm.at[head], e_ref.at[head], sem.at[head])

    loaded(0).start()
    loaded(1).start()
    predicted = part_ref[...] + other_ref[...].astype(F32)
    gp = (mask_ref[...].astype(F32) * predicted - held_ref[...].astype(F32)) * loss_weight
    gp2 = rows_cat(gp, gp)
    turned = gp2.T.astype(BF16)
    a_ref[...] = dot(at_ref[...], gp2.astype(BF16)).astype(BF16)
    hi, lo = split(c_ref[...])
    n = dot(hi, turned) + dot(lo, turned)
    for p in range(n.shape[0] // pair):
        even, odd = n[p * pair : p * pair + vox], n[p * pair + vox : (p + 1) * pair]
        sums_ref[vox:, p * pair : (p + 1) * pair] = jnp.where(left, even, odd)

    for head in range(2, min(4, heads)):
        loaded(head).start()

    @pl.loop(0, heads // 2)
    def _(step):
        loaded(2 * step).wait()
        loaded(2 * step + 1).wait()

        @pl.when(step < heads // 2 - 2)
        def _():
            loaded(2 * step + 4).start()
            loaded(2 * step + 5).start()

        ms = []
        for i in range(2):
            here = pl.ds(pl.multiple_of((2 * step + i) * vox, vox), vox)
            a = a_ref[here, :]
            c = c_ref[here, :]
            off = jnp.sum(a.astype(F32) * c, 0, keepdims=True)
            t = dot(u_ref[...], rows_cat(a, a)) - off
            ds = (e_ref[2 * step + i].astype(F32) * t).astype(BF16)
            x = dot(ut_ref[:pair, :], ds)
            x = (x[:vox] + x[vox:]) * (inv_ref[2 * step + i, :1] * factor)
            m = dot(rows_cat(*split(x)), u_ref[:rows, :])
            m = m[:vox] + m[vox:]
            ms.append(m + pltpu.roll(m, vox, 1))
        here = pl.ds(pl.multiple_of(step * pair, pair), pair)
        sums_ref[:vox, here] = jnp.where(left, ms[0], ms[1])


def final_kernel(seq_axis, mine_ref, other_ref, terms_ref, rows_ref, qkv_ref, out_ref):
    vox = mine_ref.shape[0]
    odd = lax.axis_index(seq_axis) % 2 == 1
    pair = 2 * vox
    left = left_half((vox, pair))

    def row_form(x, e2):
        e2 = e2.astype(F32)
        e_hi, e_lo = by_head(e2[:vox]).astype(BF16), by_head(e2[vox:]).astype(BF16)
        hi, lo = split(x)
        return dot(lanes_cat(hi, lo, hi), rows_cat(e_hi, e_hi, e_lo))

    def col_form(x, e2):
        turned = rows_cat(x, x).T
        hi = turned.astype(BF16).astype(F32)
        parts = jnp.where(left_half(turned.shape), hi, turned - hi).astype(BF16)
        e_hi, e_lo = e2[:vox], e2[vox:]
        both = dot(lanes_cat(parts, parts), rows_cat(e_hi, e_hi, e_lo, e_lo))
        return jnp.where(left, both[:vox], both[vox:])

    terms = [[], [], [], []]
    for p in range(mine_ref.shape[1] // pair):
        cols = slice(p * pair, (p + 1) * pair)
        mine, other = mine_ref[:, cols], other_ref[:, cols]
        m, n = jnp.where(odd, other, mine), jnp.where(odd, mine, other)
        terms[0].append(col_form(m, terms_ref[1, :, cols]))
        terms[1].append(row_form(m, terms_ref[0, :, cols]))
        terms[2].append(row_form(n, terms_ref[3, :, cols]))
        terms[3].append(col_form(n, terms_ref[2, :, cols]))
    for j in range(3):
        qkv_ref[j] = dot(rows_ref[0], rows_cat(*split(lanes_cat(*terms[j]))))
    out_ref[...] = dot(rows_ref[1], rows_cat(*split(lanes_cat(*terms[3]))))


def shifted(x, axis, mask):
    return lax.ppermute(x, axis, [(i, i ^ mask) for i in range(lax.axis_size(axis))])


def sum_over(x, axis):
    half = x.shape[0] // 2
    odd = lax.axis_index(axis) % 2 == 1
    top, bottom = x[:half], x[half:]
    mine = jnp.where(odd, bottom, top) + shifted(jnp.where(odd, top, bottom), axis, 1)
    bits = [1 << b for b in range(1, lax.axis_size(axis).bit_length() - 1)]
    groups = [bits[:2]] + [[b] for b in bits[2:]]
    for group in groups:
        masks = [0]
        for b in group:
            masks += [m ^ b for m in masks]
        sent = mine.astype(BF16)
        parts = [mine] + [shifted(sent, axis, m).astype(F32) for m in masks[1:]]
        mine = functools.reduce(jnp.add, parts)
    return mine, shifted(mine, axis, 1)


def in_hbm(x):
    return pltpu.with_memory_space_constraint(x, pltpu.MemorySpace.HBM)


def struct(shape, dtype):
    return jax.ShapeDtypeStruct(shape, dtype)


def per_device(volume, vox_mask, embed, w_qkv, w_out, w_head):
    rows, vox = volume.shape
    dim, width = w_qkv.shape[1:]
    heads = width // vox
    pair = 2 * vox
    factor = (dim // HEADS) ** (-0.5)
    seq = lax.axis_size("seq")
    keys = (LEVELS + 1) * rows
    loss_weight = 256.0 / math.sqrt(rows * seq)

    vol_t, mask_t, head_t = volume.T, vox_mask.T, w_head.T
    mask = mask_t.astype(BF16)
    kept, held, mask = lax.optimization_barrier((vol_t * (1 - mask_t).astype(BF16), vol_t * mask, mask))
    others = [shifted(kept, "seq", 1 << bit) for bit in range(LEVELS)]
    piece = dim // seq

    hbm = pl.BlockSpec(memory_space=pltpu.MemorySpace.HBM)
    vmem = pl.BlockSpec(memory_space=pltpu.MemorySpace.VMEM)
    q, ut0, u0, ah, terms, own, embed_t = pl.pallas_call(
        functools.partial(weights_kernel, factor * math.log2(math.e)),
        in_specs=[vmem] + [hbm] * 4,
        out_specs=[vmem] * 7,
        out_shape=(
            struct((width, rows), BF16),
            struct((pair, rows), BF16),
            struct((rows, pair), BF16),
            struct((pair, width), BF16),
            struct((4, pair, width), BF16),
            struct((vox, pair), BF16),
            struct((dim, vox), BF16),
        ),
        scratch_shapes=[
            pltpu.VMEM((vox, dim), BF16),
            pltpu.VMEM((vox, dim), BF16),
            pltpu.VMEM((4, dim, width), BF16),
            pltpu.SemaphoreType.DMA((6,)),
        ],
        name="weights",
        compiler_params=pltpu.CompilerParams(vmem_limit_bytes=24 * MIB),
    )(kept, in_hbm(embed), in_hbm(head_t), in_hbm(w_qkv), in_hbm(w_out))

    e, c, inv, part, sent, u, ut = pl.pallas_call(
        forward_kernel,
        in_specs=[vmem] * 9,
        out_specs=(hbm,) + (vmem,) * 6,
        out_shape=(
            pltpu.MemorySpace.HBM((heads, keys, rows), BF16),
            struct((width, rows), F32),
            struct((heads, 8, rows), F32),
            struct((vox, rows), F32),
            struct((vox, rows), BF16),
            struct((keys, pair), BF16),
            struct((pair + ONES, keys), BF16),
        ),
        scratch_shapes=[
            pltpu.VMEM((keys, rows), F32),
            pltpu.VMEM((keys, rows), F32),
            pltpu.VMEM((8, rows), F32),
            pltpu.VMEM((heads, keys, rows), BF16),
            pltpu.SemaphoreType.DMA((heads - 1,)),
            pltpu.SemaphoreType.DMA((keys // min(256, rows),)),
        ],
        name="forward",
        compiler_params=pltpu.CompilerParams(vmem_limit_bytes=FWD_MIB * MIB),
    )(kept, ut0, u0, *others, embed_t, q, ah, own)

    other = shifted(sent, "head", 1)

    at, picked = pl.pallas_call(
        functools.partial(late_kernel, "seq", piece),
        in_specs=[vmem] * 2 + [hbm] * 2,
        out_specs=[vmem] * 2,
        out_shape=(struct((width, pair), BF16), struct((2, piece, pair), BF16)),
        scratch_shapes=[
            pltpu.VMEM((vox, dim), BF16),
            pltpu.VMEM((vox, dim), BF16),
            pltpu.SemaphoreType.DMA((2,)),
        ],
        name="late",
        cost_estimate=pl.CostEstimate(flops=4 * width * dim * vox, bytes_accessed=4 * MIB, transcendentals=0),
        compiler_params=pltpu.CompilerParams(vmem_limit_bytes=8 * MIB),
    )(sent, terms, in_hbm(embed), in_hbm(head_t))

    sums = pl.pallas_call(
        functools.partial(backward_kernel, loss_weight, factor),
        in_specs=[vmem] * 7 + [hbm] + [vmem] * 2,
        out_specs=vmem,
        out_shape=struct((pair, width), F32),
        scratch_shapes=[
            pltpu.VMEM((width, rows), BF16),
            pltpu.VMEM((heads, keys, rows), BF16),
            pltpu.SemaphoreType.DMA((heads,)),
        ],
        name="backward",
        compiler_params=pltpu.CompilerParams(vmem_limit_bytes=BWD_MIB * MIB),
    )(part, other, held, mask, at, c, inv, in_hbm(e), u, ut)

    mine, swapped = sum_over(sums, "seq")
    return pl.pallas_call(
        functools.partial(final_kernel, "seq"),
        out_shape=(struct((3, piece, width), F32), struct((piece, width), F32)),
        name="final",
        compiler_params=pltpu.CompilerParams(vmem_limit_bytes=8 * MIB),
    )(mine, swapped, terms, picked)


def solution(mesh):
    return jax.shard_map(
        per_device,
        mesh=mesh,
        in_specs=(P("seq", None), P("seq", None), P(), P(None, None, "head"), P(None, "head"), P()),
        out_specs=(P(None, "seq", "head"), P("seq", "head")),
        check_vma=False,
    )
```

```python
import functools
import math

import jax
import jax.numpy as jnp
from jax import lax
from jax.experimental import pallas as pl
from jax.experimental.pallas import tpu as pltpu
from jax.sharding import PartitionSpec as P

HEADS = 16
LEVELS = 2
F32 = jnp.float32
BF16 = jnp.bfloat16
ONES = 16
MIB = 1 << 20
FWD_MIB = 34
BWD_MIB = 34


def dot(a, b):
    return jnp.dot(a, b, preferred_element_type=F32)


def dot_nt(a, b):
    return lax.dot_general(a, b, (((1,), (1,)), ((), ())), preferred_element_type=F32)


def split(x):
    high = x.astype(BF16)
    return high, (x - high.astype(F32)).astype(BF16)


def rows_cat(*parts):
    return jnp.concatenate(parts, 0)


def lanes_cat(*parts):
    return jnp.concatenate(parts, 1)


def left_half(shape):
    return lax.broadcasted_iota(jnp.int32, shape, 1) < shape[1] // 2


def top_half(shape):
    return lax.broadcasted_iota(jnp.int32, shape, 0) < shape[0] // 2


def by_head(pair):
    left = left_half(pair.shape)
    return rows_cat(jnp.where(left, pair, 0.0), jnp.where(left, 0.0, pair))


def product(x, y):
    x_hi, x_lo = split(x)
    y_hi, y_lo = split(y)
    return dot_nt(lanes_cat(x_hi, x_lo), lanes_cat(y_hi, y_hi)) + dot_nt(x_hi, y_lo)


def unit_rows(kept, embed_t):
    hidden = dot(embed_t, kept)
    rms = lax.rsqrt(jnp.sum(hidden * hidden, 0, keepdims=True) / embed_t.shape[0] + 1e-06)
    hi, lo = split(kept.astype(F32) * rms)
    return rows_cat(hi, lo), rows_cat(hi.astype(F32), lo.astype(F32)).T.astype(BF16)


def weights_kernel(
    scale, kept_ref, embed_hbm, head_t_hbm, w_qkv_hbm, w_out_hbm,
    q_ref, ut_ref, u_ref, ah_ref, terms_ref, own_ref, embed_t_ref,
    embed_ref, head_t_ref, w_ref, sem,
):
    small = [pltpu.make_async_copy(embed_hbm, embed_ref, sem.at[4])]
    small.append(pltpu.make_async_copy(head_t_hbm, head_t_ref, sem.at[5]))
    for copy in small:
        copy.start()
    copies = [pltpu.make_async_copy(w_qkv_hbm.at[j], w_ref.at[j], sem.at[j]) for j in range(3)]
    copies.append(pltpu.make_async_copy(w_out_hbm, w_ref.at[3], sem.at[3]))
    for copy in copies:
        copy.start()
    for copy in small:
        copy.wait()
    embed = embed_ref[...]
    head_t = head_t_ref[...]
    embed_t = embed.astype(F32).T.astype(BF16)
    embed_t_ref[...] = embed_t
    both, u_ref[...] = unit_rows(kept_ref[...], embed_t)
    ut_ref[...] = both
    own = dot_nt(head_t, embed)
    own_hi, own_lo = split(own)
    own_ref[...] = lanes_cat(own_hi, own_lo)
    pair = 2 * embed.shape[0]
    copies[0].wait()
    eq = dot(embed, w_ref[0])
    copies[1].wait()
    ek = dot(embed, w_ref[1])
    pairs = [slice(p * pair, (p + 1) * pair) for p in range(eq.shape[1] // pair)]
    for here in pairs:
        q, k = eq[:, here], ek[:, here]
        b = product(by_head(k), rows_cat(q, q) * scale)
        q_ref[here, :] = dot(lanes_cat(*split(b)), rows_cat(both, both)).astype(BF16)
        terms_ref[0, :, here] = rows_cat(*split(q))
        terms_ref[1, :, here] = rows_cat(*split(k))
    copies[2].wait()
    ev = dot(embed, w_ref[2])
    copies[3].wait()
    gt = dot(head_t, w_ref[3])
    for here in pairs:
        v, g = ev[:, here], gt[:, here]
        v2, g2 = by_head(v), rows_cat(g, g)
        a = product(g2, v2)
        hi, lo = split(a)
        ah_ref[:, here] = jnp.where(top_half(a.shape), hi.astype(F32), lo.astype(F32)).astype(BF16)
        terms_ref[2, :, here] = rows_cat(*split(v))
        terms_ref[3, :, here] = rows_cat(*split(g))


def late_kernel(seq_axis, piece, after_ref, terms_ref, embed_hbm, head_t_hbm, at_ref, rows_ref, embed_ref, head_t_ref, sem):
    copies = [pltpu.make_async_copy(embed_hbm, embed_ref, sem.at[0])]
    copies.append(pltpu.make_async_copy(head_t_hbm, head_t_ref, sem.at[1]))
    for copy in copies:
        copy.start()
    vox = embed_ref.shape[0]
    pair = 2 * vox
    for p in range(terms_ref.shape[2] // pair):
        here = slice(p * pair, (p + 1) * pair)
        v, g = terms_ref[2, :, here].astype(F32), terms_ref[3, :, here]
        v_hi, v_lo = by_head(v[:vox]).astype(BF16), by_head(v[vox:]).astype(BF16)
        g_hi, g_lo = rows_cat(g[:vox], g[:vox]), rows_cat(g[vox:], g[vox:])
        a = dot_nt(lanes_cat(v_hi, v_lo), lanes_cat(g_hi, g_hi)) + dot_nt(v_hi, g_lo)
        hi = a.astype(BF16).astype(F32)
        at_ref[here, :] = jnp.where(left_half(a.shape), hi, a - hi).astype(BF16)
    for copy in copies:
        copy.wait()
    first = lax.axis_index(seq_axis) * piece
    shape = (piece, embed_ref.shape[1])
    wanted = lax.broadcasted_iota(jnp.int32, shape, 0) + first == lax.broadcasted_iota(jnp.int32, shape, 1)
    pick = jnp.where(wanted, 1.0, 0.0).astype(BF16)
    for j, ref in enumerate((embed_ref, head_t_ref)):
        rows_ref[j] = dot_nt(pick, rows_cat(ref[...], ref[...])).astype(BF16)


def forward_kernel(
    kept_ref, ut0_ref, u0_ref, k1_ref, k2_ref, embed_t_ref, q_ref, ah_ref, own_ref,
    e_hbm, c_ref, inv_ref, part_ref, sent_ref, u_ref, ut_ref,
    s0_ref, s1_ref, top_ref, e_ref, sem, last_sem,
):
    vox, rows = kept_ref.shape
    heads, keys = e_ref.shape[:2]
    pair = 2 * vox
    chunk = min(256, rows)
    chunks = [slice(j * chunk, (j + 1) * chunk) for j in range(keys // chunk)]

    def stored(head):
        return pltpu.make_async_copy(e_ref.at[head], e_hbm.at[head], sem.at[head])

    def piece(j):
        here = (heads - 1, pl.ds(j * chunk, chunk))
        return pltpu.make_async_copy(e_ref.at[here], e_hbm.at[here], last_sem.at[j])

    embed_t = embed_t_ref[...]
    blocks = [(ut0_ref[...], u0_ref[...])] + [unit_rows(ref[...], embed_t) for ref in (k1_ref, k2_ref)]
    for j, (both, turned) in enumerate(blocks):
        here = slice(j * rows, (j + 1) * rows)
        ut_ref[:pair, here] = both
        ut_ref[pair:, here] = jnp.ones((ONES, rows), BF16)
        u_ref[here, :] = turned

    def scores(head, s_ref):
        q = q_ref[pl.ds(pl.multiple_of(head * vox, vox), vox), :]
        q = rows_cat(q, q)
        top = None
        for here in chunks:
            s = dot(u_ref[here, :], q)
            s_ref[here, :] = s
            highest = jnp.max(s.reshape(chunk // 8, 8, rows), 0)
            top = highest if top is None else jnp.maximum(top, highest)
        return top

    def softmax(head, s_ref, top, leave=False):
        top = jnp.max(top, 0, keepdims=True)
        for j, here in enumerate(chunks):
            e_ref[head, here, :] = jnp.exp2(s_ref[here, :] - top).astype(BF16)
            if leave:
                piece(j).start()
        c = dot(ut_ref[...], e_ref[head])
        inv = 1.0 / c[pair : pair + 8]
        inv_ref[head] = inv
        c_ref[pl.ds(pl.multiple_of(head * vox, vox), vox), :] = (c[:vox] + c[vox:pair]) * inv[:1]

    top_ref[...] = scores(0, s0_ref)

    def both_of(head, now_ref, next_ref):
        top = top_ref[...]
        top_ref[...] = scores(head + 1, next_ref)
        softmax(head, now_ref, top)

    @pl.loop(0, heads - 1)
    def _(head):
        @pl.when(head % 2 == 0)
        def _():
            both_of(head, s0_ref, s1_ref)

        @pl.when(head % 2 == 1)
        def _():
            both_of(head, s1_ref, s0_ref)

        stored(head).start()

    softmax(heads - 1, s1_ref if heads % 2 == 0 else s0_ref, top_ref[...], True)
    hi, lo = split(c_ref[...])
    ah = ah_ref[...]
    p2 = dot(ah, hi)
    part = p2[:vox] + p2[vox:] + dot(ah[:vox], lo)
    sent_ref[...] = part.astype(BF16)
    kept = kept_ref[...]
    part_ref[...] = part + dot(own_ref[...], rows_cat(kept, kept))
    for head in range(heads - 1):
        stored(head).wait()
    for j in range(len(chunks)):
        piece(j).wait()


def backward_kernel(
    loss_weight, factor,
    part_ref, other_ref, held_ref, mask_ref, at_ref, c_ref, inv_ref, e_hbm, u_ref, ut_ref,
    sums_ref,
    a_ref, e_ref, sem,
):
    vox, rows = held_ref.shape
    heads = e_ref.shape[0]
    pair = 2 * vox
    left = left_half((vox, pair))

    def loaded(head):
        return pltpu.make_async_copy(e_hbm.at[head], e_ref.at[head], sem.at[head])

    loaded(0).start()
    loaded(1).start()
    predicted = part_ref[...] + other_ref[...].astype(F32)
    gp = (mask_ref[...].astype(F32) * predicted - held_ref[...].astype(F32)) * loss_weight
    gp2 = rows_cat(gp, gp)
    turned = gp2.T.astype(BF16)
    a_ref[...] = dot(at_ref[...], gp2.astype(BF16)).astype(BF16)
    hi, lo = split(c_ref[...])
    n = dot(hi, turned) + dot(lo, turned)
    for p in range(n.shape[0] // pair):
        even, odd = n[p * pair : p * pair + vox], n[p * pair + vox : (p + 1) * pair]
        sums_ref[vox:, p * pair : (p + 1) * pair] = jnp.where(left, even, odd)

    for head in range(2, min(4, heads)):
        loaded(head).start()

    @pl.loop(0, heads // 2)
    def _(step):
        loaded(2 * step).wait()
        loaded(2 * step + 1).wait()

        @pl.when(step < heads // 2 - 2)
        def _():
            loaded(2 * step + 4).start()
            loaded(2 * step + 5).start()

        ms = []
        for i in range(2):
            here = pl.ds(pl.multiple_of((2 * step + i) * vox, vox), vox)
            a = a_ref[here, :]
            c = c_ref[here, :]
            off = jnp.sum(a.astype(F32) * c, 0, keepdims=True)
            t = dot(u_ref[...], rows_cat(a, a)) - off
            ds = (e_ref[2 * step + i].astype(F32) * t).astype(BF16)
            x = dot(ut_ref[:pair, :], ds)
            x = (x[:vox] + x[vox:]) * (inv_ref[2 * step + i, :1] * factor)
            m = dot(rows_cat(*split(x)), u_ref[:rows, :])
            m = m[:vox] + m[vox:]
            ms.append(m + pltpu.roll(m, vox, 1))
        here = pl.ds(pl.multiple_of(step * pair, pair), pair)
        sums_ref[:vox, here] = jnp.where(left, ms[0], ms[1])


def final_kernel(seq_axis, mine_ref, other_ref, terms_ref, rows_ref, qkv_ref, out_ref):
    vox = mine_ref.shape[0]
    odd = lax.axis_index(seq_axis) % 2 == 1
    pair = 2 * vox
    left = left_half((vox, pair))

    def row_form(x, e2):
        e2 = e2.astype(F32)
        e_hi, e_lo = by_head(e2[:vox]).astype(BF16), by_head(e2[vox:]).astype(BF16)
        hi, lo = split(x)
        return dot(lanes_cat(hi, lo, hi), rows_cat(e_hi, e_hi, e_lo))

    def col_form(x, e2):
        turned = rows_cat(x, x).T
        hi = turned.astype(BF16).astype(F32)
        parts = jnp.where(left_half(turned.shape), hi, turned - hi).astype(BF16)
        e_hi, e_lo = e2[:vox], e2[vox:]
        both = dot(lanes_cat(parts, parts), rows_cat(e_hi, e_hi, e_lo, e_lo))
        return jnp.where(left, both[:vox], both[vox:])

    terms = [[], [], [], []]
    for p in range(mine_ref.shape[1] // pair):
        cols = slice(p * pair, (p + 1) * pair)
        mine, other = mine_ref[:, cols], other_ref[:, cols]
        m, n = jnp.where(odd, other, mine), jnp.where(odd, mine, other)
        terms[0].append(col_form(m, terms_ref[1, :, cols]))
        terms[1].append(row_form(m, terms_ref[0, :, cols]))
        terms[2].append(row_form(n, terms_ref[3, :, cols]))
        terms[3].append(col_form(n, terms_ref[2, :, cols]))
    for j in range(3):
        qkv_ref[j] = dot(rows_ref[0], rows_cat(*split(lanes_cat(*terms[j]))))
    out_ref[...] = dot(rows_ref[1], rows_cat(*split(lanes_cat(*terms[3]))))


def shifted(x, axis, mask):
    return lax.ppermute(x, axis, [(i, i ^ mask) for i in range(lax.axis_size(axis))])


def sum_over(x, axis):
    half = x.shape[0] // 2
    odd = lax.axis_index(axis) % 2 == 1
    top, bottom = x[:half], x[half:]
    mine = jnp.where(odd, bottom, top) + shifted(jnp.where(odd, top, bottom), axis, 1)
    bits = [1 << b for b in range(1, lax.axis_size(axis).bit_length() - 1)]
    groups = [bits[:2]] + [[b] for b in bits[2:]]
    for group in groups:
        masks = [0]
        for b in group:
            masks += [m ^ b for m in masks]
        sent = mine.astype(BF16)
        parts = [mine] + [shifted(sent, axis, m).astype(F32) for m in reversed(masks[1:])]
        mine = functools.reduce(jnp.add, parts)
    return mine, shifted(mine, axis, 1)


def in_hbm(x):
    return pltpu.with_memory_space_constraint(x, pltpu.MemorySpace.HBM)


def struct(shape, dtype):
    return jax.ShapeDtypeStruct(shape, dtype)


def per_device(volume, vox_mask, embed, w_qkv, w_out, w_head):
    rows, vox = volume.shape
    dim, width = w_qkv.shape[1:]
    heads = width // vox
    pair = 2 * vox
    factor = (dim // HEADS) ** (-0.5)
    seq = lax.axis_size("seq")
    keys = (LEVELS + 1) * rows
    loss_weight = 256.0 / math.sqrt(rows * seq)

    vol_t, mask_t, head_t = volume.T, vox_mask.T, w_head.T
    mask = mask_t.astype(BF16)
    kept, held, mask = lax.optimization_barrier((vol_t * (1 - mask_t).astype(BF16), vol_t * mask, mask))
    others = [shifted(kept, "seq", 1 << bit) for bit in range(LEVELS)]
    piece = dim // seq

    hbm = pl.BlockSpec(memory_space=pltpu.MemorySpace.HBM)
    vmem = pl.BlockSpec(memory_space=pltpu.MemorySpace.VMEM)
    q, ut0, u0, ah, terms, own, embed_t = pl.pallas_call(
        functools.partial(weights_kernel, factor * math.log2(math.e)),
        in_specs=[vmem] + [hbm] * 4,
        out_specs=[vmem] * 7,
        out_shape=(
            struct((width, rows), BF16),
            struct((pair, rows), BF16),
            struct((rows, pair), BF16),
            struct((pair, width), BF16),
            struct((4, pair, width), BF16),
            struct((vox, pair), BF16),
            struct((dim, vox), BF16),
        ),
        scratch_shapes=[
            pltpu.VMEM((vox, dim), BF16),
            pltpu.VMEM((vox, dim), BF16),
            pltpu.VMEM((4, dim, width), BF16),
            pltpu.SemaphoreType.DMA((6,)),
        ],
        name="weights",
        compiler_params=pltpu.CompilerParams(vmem_limit_bytes=24 * MIB),
    )(kept, in_hbm(embed), in_hbm(head_t), in_hbm(w_qkv), in_hbm(w_out))

    e, c, inv, part, sent, u, ut = pl.pallas_call(
        forward_kernel,
        in_specs=[vmem] * 9,
        out_specs=(hbm,) + (vmem,) * 6,
        out_shape=(
            pltpu.MemorySpace.HBM((heads, keys, rows), BF16),
            struct((width, rows), F32),
            struct((heads, 8, rows), F32),
            struct((vox, rows), F32),
            struct((vox, rows), BF16),
            struct((keys, pair), BF16),
            struct((pair + ONES, keys), BF16),
        ),
        scratch_shapes=[
            pltpu.VMEM((keys, rows), F32),
            pltpu.VMEM((keys, rows), F32),
            pltpu.VMEM((8, rows), F32),
            pltpu.VMEM((heads, keys, rows), BF16),
            pltpu.SemaphoreType.DMA((heads - 1,)),
            pltpu.SemaphoreType.DMA((keys // min(256, rows),)),
        ],
        name="forward",
        compiler_params=pltpu.CompilerParams(vmem_limit_bytes=FWD_MIB * MIB),
    )(kept, ut0, u0, *others, embed_t, q, ah, own)

    other = shifted(sent, "head", 1)

    at, picked = pl.pallas_call(
        functools.partial(late_kernel, "seq", piece),
        in_specs=[vmem] * 2 + [hbm] * 2,
        out_specs=[vmem] * 2,
        out_shape=(struct((width, pair), BF16), struct((2, piece, pair), BF16)),
        scratch_shapes=[
            pltpu.VMEM((vox, dim), BF16),
            pltpu.VMEM((vox, dim), BF16),
            pltpu.SemaphoreType.DMA((2,)),
        ],
        name="late",
        cost_estimate=pl.CostEstimate(flops=4 * width * dim * vox, bytes_accessed=4 * MIB, transcendentals=0),
        compiler_params=pltpu.CompilerParams(vmem_limit_bytes=8 * MIB),
    )(sent, terms, in_hbm(embed), in_hbm(head_t))

    sums = pl.pallas_call(
        functools.partial(backward_kernel, loss_weight, factor),
        in_specs=[vmem] * 7 + [hbm] + [vmem] * 2,
        out_specs=vmem,
        out_shape=struct((pair, width), F32),
        scratch_shapes=[
            pltpu.VMEM((width, rows), BF16),
            pltpu.VMEM((heads, keys, rows), BF16),
            pltpu.SemaphoreType.DMA((heads,)),
        ],
        name="backward",
        compiler_params=pltpu.CompilerParams(vmem_limit_bytes=BWD_MIB * MIB),
    )(part, other, held, mask, at, c, inv, in_hbm(e), u, ut)

    mine, swapped = sum_over(sums, "seq")
    return pl.pallas_call(
        functools.partial(final_kernel, "seq"),
        out_shape=(struct((3, piece, width), F32), struct((piece, width), F32)),
        name="final",
        compiler_params=pltpu.CompilerParams(vmem_limit_bytes=8 * MIB),
    )(mine, swapped, terms, picked)


def solution(mesh):
    return jax.shard_map(
        per_device,
        mesh=mesh,
        in_specs=(P("seq", None), P("seq", None), P(), P(None, None, "head"), P(None, "head"), P()),
        out_specs=(P(None, "seq", "head"), P("seq", "head")),
        check_vma=False,
    )
```

```python
import functools
import math

import jax
import jax.numpy as jnp
from jax import lax
from jax.experimental import pallas as pl
from jax.experimental.pallas import tpu as pltpu
from jax.sharding import PartitionSpec as P

HEADS = 16
LEVELS = 2
F32 = jnp.float32
BF16 = jnp.bfloat16
ONES = 16
MIB = 1 << 20
FWD_MIB = 34
BWD_MIB = 34


def dot(a, b):
    return jnp.dot(a, b, preferred_element_type=F32)


def dot_nt(a, b):
    return lax.dot_general(a, b, (((1,), (1,)), ((), ())), preferred_element_type=F32)


def split(x):
    high = x.astype(BF16)
    return high, (x - high.astype(F32)).astype(BF16)


def rows_cat(*parts):
    return jnp.concatenate(parts, 0)


def lanes_cat(*parts):
    return jnp.concatenate(parts, 1)


def left_half(shape):
    return lax.broadcasted_iota(jnp.int32, shape, 1) < shape[1] // 2


def top_half(shape):
    return lax.broadcasted_iota(jnp.int32, shape, 0) < shape[0] // 2


def by_head(pair):
    left = left_half(pair.shape)
    return rows_cat(jnp.where(left, pair, 0.0), jnp.where(left, 0.0, pair))


def product(x, y):
    x_hi, x_lo = split(x)
    y_hi, y_lo = split(y)
    return dot_nt(lanes_cat(x_hi, x_lo), lanes_cat(y_hi, y_hi)) + dot_nt(x_hi, y_lo)


def unit_rows(kept, embed_t):
    hidden = dot(embed_t, kept)
    rms = lax.rsqrt(jnp.sum(hidden * hidden, 0, keepdims=True) / embed_t.shape[0] + 1e-06)
    hi, lo = split(kept.astype(F32) * rms)
    return rows_cat(hi, lo), rows_cat(hi.astype(F32), lo.astype(F32)).T.astype(BF16)


def weights_kernel(
    scale, kept_ref, embed_hbm, head_t_hbm, w_qkv_hbm, w_out_hbm,
    q_ref, ut_ref, u_ref, ah_ref, terms_ref, embed_t_ref,
    embed_ref, head_t_ref, w_ref, sem,
):
    small = [pltpu.make_async_copy(embed_hbm, embed_ref, sem.at[4])]
    small.append(pltpu.make_async_copy(head_t_hbm, head_t_ref, sem.at[5]))
    for copy in small:
        copy.start()
    copies = [pltpu.make_async_copy(w_qkv_hbm.at[j], w_ref.at[j], sem.at[j]) for j in range(3)]
    copies.append(pltpu.make_async_copy(w_out_hbm, w_ref.at[3], sem.at[3]))
    for copy in copies:
        copy.start()
    for copy in small:
        copy.wait()
    embed = embed_ref[...]
    head_t = head_t_ref[...]
    embed_t = embed.astype(F32).T.astype(BF16)
    embed_t_ref[...] = embed_t
    both, u_ref[...] = unit_rows(kept_ref[...], embed_t)
    ut_ref[...] = both
    pair = 2 * embed.shape[0]
    copies[0].wait()
    eq = dot(embed, w_ref[0])
    copies[1].wait()
    ek = dot(embed, w_ref[1])
    pairs = [slice(p * pair, (p + 1) * pair) for p in range(eq.shape[1] // pair)]
    for here in pairs:
        q, k = eq[:, here], ek[:, here]
        b = product(by_head(k), rows_cat(q, q) * scale)
        q_ref[here, :] = dot(lanes_cat(*split(b)), rows_cat(both, both)).astype(BF16)
        terms_ref[0, :, here] = rows_cat(*split(q))
        terms_ref[1, :, here] = rows_cat(*split(k))
    copies[2].wait()
    ev = dot(embed, w_ref[2])
    copies[3].wait()
    gt = dot(head_t, w_ref[3])
    for here in pairs:
        v, g = ev[:, here], gt[:, here]
        v2, g2 = by_head(v), rows_cat(g, g)
        a = product(g2, v2)
        hi, lo = split(a)
        ah_ref[:, here] = jnp.where(top_half(a.shape), hi.astype(F32), lo.astype(F32)).astype(BF16)
        terms_ref[2, :, here] = rows_cat(*split(v))
        terms_ref[3, :, here] = rows_cat(*split(g))


def late_kernel(seq_axis, piece, after_ref, terms_ref, embed_hbm, head_t_hbm, at_ref, rows_ref, own_ref, embed_ref, head_t_ref, sem):
    copies = [pltpu.make_async_copy(embed_hbm, embed_ref, sem.at[0])]
    copies.append(pltpu.make_async_copy(head_t_hbm, head_t_ref, sem.at[1]))
    for copy in copies:
        copy.start()
    vox = embed_ref.shape[0]
    pair = 2 * vox
    for p in range(terms_ref.shape[2] // pair):
        here = slice(p * pair, (p + 1) * pair)
        v, g = terms_ref[2, :, here].astype(F32), terms_ref[3, :, here]
        v_hi, v_lo = by_head(v[:vox]).astype(BF16), by_head(v[vox:]).astype(BF16)
        g_hi, g_lo = rows_cat(g[:vox], g[:vox]), rows_cat(g[vox:], g[vox:])
        a = dot_nt(lanes_cat(v_hi, v_lo), lanes_cat(g_hi, g_hi)) + dot_nt(v_hi, g_lo)
        hi = a.astype(BF16).astype(F32)
        at_ref[here, :] = jnp.where(left_half(a.shape), hi, a - hi).astype(BF16)
    for copy in copies:
        copy.wait()
    own_ref[...] = lanes_cat(*split(dot_nt(head_t_ref[...], embed_ref[...])))
    first = lax.axis_index(seq_axis) * piece
    shape = (piece, embed_ref.shape[1])
    wanted = lax.broadcasted_iota(jnp.int32, shape, 0) + first == lax.broadcasted_iota(jnp.int32, shape, 1)
    pick = jnp.where(wanted, 1.0, 0.0).astype(BF16)
    for j, ref in enumerate((embed_ref, head_t_ref)):
        rows_ref[j] = dot_nt(pick, rows_cat(ref[...], ref[...])).astype(BF16)


def forward_kernel(
    kept_ref, ut0_ref, u0_ref, k1_ref, k2_ref, embed_t_ref, q_ref, ah_ref,
    e_hbm, c_ref, inv_ref, part_ref, sent_ref, u_ref, ut_ref,
    s0_ref, s1_ref, top_ref, e_ref, sem, last_sem,
):
    vox, rows = kept_ref.shape
    heads, keys = e_ref.shape[:2]
    pair = 2 * vox
    chunk = min(256, rows)
    chunks = [slice(j * chunk, (j + 1) * chunk) for j in range(keys // chunk)]

    def stored(head):
        return pltpu.make_async_copy(e_ref.at[head], e_hbm.at[head], sem.at[head])

    def piece(j):
        here = (heads - 1, pl.ds(j * chunk, chunk))
        return pltpu.make_async_copy(e_ref.at[here], e_hbm.at[here], last_sem.at[j])

    embed_t = embed_t_ref[...]
    blocks = [(ut0_ref[...], u0_ref[...])] + [unit_rows(ref[...], embed_t) for ref in (k1_ref, k2_ref)]
    for j, (both, turned) in enumerate(blocks):
        here = slice(j * rows, (j + 1) * rows)
        ut_ref[:pair, here] = both
        ut_ref[pair:, here] = jnp.ones((ONES, rows), BF16)
        u_ref[here, :] = turned

    def scores(head, s_ref):
        q = q_ref[pl.ds(pl.multiple_of(head * vox, vox), vox), :]
        q = rows_cat(q, q)
        top = None
        for here in chunks:
            s = dot(u_ref[here, :], q)
            s_ref[here, :] = s
            highest = jnp.max(s.reshape(chunk // 8, 8, rows), 0)
            top = highest if top is None else jnp.maximum(top, highest)
        return top

    def softmax(head, s_ref, top, leave=False):
        top = jnp.max(top, 0, keepdims=True)
        for j, here in enumerate(chunks):
            e_ref[head, here, :] = jnp.exp2(s_ref[here, :] - top).astype(BF16)
            if leave:
                piece(j).start()
        c = dot(ut_ref[...], e_ref[head])
        inv = 1.0 / c[pair : pair + 8]
        inv_ref[head] = inv
        c_ref[pl.ds(pl.multiple_of(head * vox, vox), vox), :] = (c[:vox] + c[vox:pair]) * inv[:1]

    top_ref[...] = scores(0, s0_ref)

    def both_of(head, now_ref, next_ref):
        top = top_ref[...]
        top_ref[...] = scores(head + 1, next_ref)
        softmax(head, now_ref, top)

    @pl.loop(0, heads - 1)
    def _(head):
        @pl.when(head % 2 == 0)
        def _():
            both_of(head, s0_ref, s1_ref)

        @pl.when(head % 2 == 1)
        def _():
            both_of(head, s1_ref, s0_ref)

        stored(head).start()

    softmax(heads - 1, s1_ref if heads % 2 == 0 else s0_ref, top_ref[...], True)
    hi, lo = split(c_ref[...])
    ah = ah_ref[...]
    p2 = dot(ah, hi)
    part = p2[:vox] + p2[vox:] + dot(ah[:vox], lo)
    sent_ref[...] = part.astype(BF16)
    part_ref[...] = part
    for head in range(heads - 1):
        stored(head).wait()
    for j in range(len(chunks)):
        piece(j).wait()


def backward_kernel(
    loss_weight, factor,
    part_ref, other_ref, held_ref, mask_ref, kept_ref, own_ref, at_ref, c_ref, inv_ref, e_hbm, u_ref, ut_ref,
    sums_ref,
    a_ref, e_ref, sem,
):
    vox, rows = held_ref.shape
    heads = e_ref.shape[0]
    pair = 2 * vox
    left = left_half((vox, pair))

    def loaded(head):
        return pltpu.make_async_copy(e_hbm.at[head], e_ref.at[head], sem.at[head])

    loaded(0).start()
    loaded(1).start()
    kept = kept_ref[...]
    predicted = dot(own_ref[...], rows_cat(kept, kept)) + (part_ref[...] + other_ref[...].astype(F32))
    gp = (mask_ref[...].astype(F32) * predicted - held_ref[...].astype(F32)) * loss_weight
    gp2 = rows_cat(gp, gp)
    turned = gp2.T.astype(BF16)
    a_ref[...] = dot(at_ref[...], gp2.astype(BF16)).astype(BF16)
    hi, lo = split(c_ref[...])
    n = dot(hi, turned) + dot(lo, turned)
    for p in range(n.shape[0] // pair):
        even, odd = n[p * pair : p * pair + vox], n[p * pair + vox : (p + 1) * pair]
        sums_ref[vox:, p * pair : (p + 1) * pair] = jnp.where(left, even, odd)

    for head in range(2, min(4, heads)):
        loaded(head).start()

    @pl.loop(0, heads // 2)
    def _(step):
        loaded(2 * step).wait()
        loaded(2 * step + 1).wait()

        @pl.when(step < heads // 2 - 2)
        def _():
            loaded(2 * step + 4).start()
            loaded(2 * step + 5).start()

        ms = []
        for i in range(2):
            here = pl.ds(pl.multiple_of((2 * step + i) * vox, vox), vox)
            a = a_ref[here, :]
            c = c_ref[here, :]
            off = jnp.sum(a.astype(F32) * c, 0, keepdims=True)
            t = dot(u_ref[...], rows_cat(a, a)) - off
            ds = (e_ref[2 * step + i].astype(F32) * t).astype(BF16)
            x = dot(ut_ref[:pair, :], ds)
            x = (x[:vox] + x[vox:]) * (inv_ref[2 * step + i, :1] * factor)
            m = dot(rows_cat(*split(x)), u_ref[:rows, :])
            m = m[:vox] + m[vox:]
            ms.append(m + pltpu.roll(m, vox, 1))
        here = pl.ds(pl.multiple_of(step * pair, pair), pair)
        sums_ref[:vox, here] = jnp.where(left, ms[0], ms[1])


def final_kernel(seq_axis, mine_ref, other_ref, terms_ref, rows_ref, qkv_ref, out_ref):
    vox = mine_ref.shape[0]
    odd = lax.axis_index(seq_axis) % 2 == 1
    pair = 2 * vox
    left = left_half((vox, pair))

    def row_form(x, e2):
        e2 = e2.astype(F32)
        e_hi, e_lo = by_head(e2[:vox]).astype(BF16), by_head(e2[vox:]).astype(BF16)
        hi, lo = split(x)
        return dot(lanes_cat(hi, lo, hi), rows_cat(e_hi, e_hi, e_lo))

    def col_form(x, e2):
        turned = rows_cat(x, x).T
        hi = turned.astype(BF16).astype(F32)
        parts = jnp.where(left_half(turned.shape), hi, turned - hi).astype(BF16)
        e_hi, e_lo = e2[:vox], e2[vox:]
        both = dot(lanes_cat(parts, parts), rows_cat(e_hi, e_hi, e_lo, e_lo))
        return jnp.where(left, both[:vox], both[vox:])

    terms = [[], [], [], []]
    for p in range(mine_ref.shape[1] // pair):
        cols = slice(p * pair, (p + 1) * pair)
        mine, other = mine_ref[:, cols], other_ref[:, cols]
        m, n = jnp.where(odd, other, mine), jnp.where(odd, mine, other)
        terms[0].append(col_form(m, terms_ref[1, :, cols]))
        terms[1].append(row_form(m, terms_ref[0, :, cols]))
        terms[2].append(row_form(n, terms_ref[3, :, cols]))
        terms[3].append(col_form(n, terms_ref[2, :, cols]))
    for j in range(3):
        qkv_ref[j] = dot(rows_ref[0], rows_cat(*split(lanes_cat(*terms[j]))))
    out_ref[...] = dot(rows_ref[1], rows_cat(*split(lanes_cat(*terms[3]))))


def shifted(x, axis, mask):
    return lax.ppermute(x, axis, [(i, i ^ mask) for i in range(lax.axis_size(axis))])


def sum_over(x, axis):
    half = x.shape[0] // 2
    odd = lax.axis_index(axis) % 2 == 1
    top, bottom = x[:half], x[half:]
    mine = jnp.where(odd, bottom, top) + shifted(jnp.where(odd, top, bottom), axis, 1)
    bits = [1 << b for b in range(1, lax.axis_size(axis).bit_length() - 1)]
    groups = [bits[:2]] + [[b] for b in bits[2:]]
    for group in groups:
        masks = [0]
        for b in group:
            masks += [m ^ b for m in masks]
        sent = mine.astype(BF16)
        parts = [mine] + [shifted(sent, axis, m).astype(F32) for m in reversed(masks[1:])]
        mine = functools.reduce(jnp.add, parts)
    return mine, shifted(mine, axis, 1)


def in_hbm(x):
    return pltpu.with_memory_space_constraint(x, pltpu.MemorySpace.HBM)


def struct(shape, dtype):
    return jax.ShapeDtypeStruct(shape, dtype)


def per_device(volume, vox_mask, embed, w_qkv, w_out, w_head):
    rows, vox = volume.shape
    dim, width = w_qkv.shape[1:]
    heads = width // vox
    pair = 2 * vox
    factor = (dim // HEADS) ** (-0.5)
    seq = lax.axis_size("seq")
    keys = (LEVELS + 1) * rows
    loss_weight = 256.0 / math.sqrt(rows * seq)

    vol_t, mask_t, head_t = volume.T, vox_mask.T, w_head.T
    mask = mask_t.astype(BF16)
    kept, held, mask = lax.optimization_barrier((vol_t * (1 - mask_t).astype(BF16), vol_t * mask, mask))
    others = [shifted(kept, "seq", 1 << bit) for bit in range(LEVELS)]
    piece = dim // seq

    hbm = pl.BlockSpec(memory_space=pltpu.MemorySpace.HBM)
    vmem = pl.BlockSpec(memory_space=pltpu.MemorySpace.VMEM)
    q, ut0, u0, ah, terms, embed_t = pl.pallas_call(
        functools.partial(weights_kernel, factor * math.log2(math.e)),
        in_specs=[vmem] + [hbm] * 4,
        out_specs=[vmem] * 6,
        out_shape=(
            struct((width, rows), BF16),
            struct((pair, rows), BF16),
            struct((rows, pair), BF16),
            struct((pair, width), BF16),
            struct((4, pair, width), BF16),
            struct((dim, vox), BF16),
        ),
        scratch_shapes=[
            pltpu.VMEM((vox, dim), BF16),
            pltpu.VMEM((vox, dim), BF16),
            pltpu.VMEM((4, dim, width), BF16),
            pltpu.SemaphoreType.DMA((6,)),
        ],
        name="weights",
        compiler_params=pltpu.CompilerParams(vmem_limit_bytes=24 * MIB),
    )(kept, in_hbm(embed), in_hbm(head_t), in_hbm(w_qkv), in_hbm(w_out))

    e, c, inv, part, sent, u, ut = pl.pallas_call(
        forward_kernel,
        in_specs=[vmem] * 8,
        out_specs=(hbm,) + (vmem,) * 6,
        out_shape=(
            pltpu.MemorySpace.HBM((heads, keys, rows), BF16),
            struct((width, rows), F32),
            struct((heads, 8, rows), F32),
            struct((vox, rows), F32),
            struct((vox, rows), BF16),
            struct((keys, pair), BF16),
            struct((pair + ONES, keys), BF16),
        ),
        scratch_shapes=[
            pltpu.VMEM((keys, rows), F32),
            pltpu.VMEM((keys, rows), F32),
            pltpu.VMEM((8, rows), F32),
            pltpu.VMEM((heads, keys, rows), BF16),
            pltpu.SemaphoreType.DMA((heads - 1,)),
            pltpu.SemaphoreType.DMA((keys // min(256, rows),)),
        ],
        name="forward",
        compiler_params=pltpu.CompilerParams(vmem_limit_bytes=FWD_MIB * MIB),
    )(kept, ut0, u0, *others, embed_t, q, ah)

    other = shifted(sent, "head", 1)

    at, picked, own = pl.pallas_call(
        functools.partial(late_kernel, "seq", piece),
        in_specs=[vmem] * 2 + [hbm] * 2,
        out_specs=[vmem] * 3,
        out_shape=(struct((width, pair), BF16), struct((2, piece, pair), BF16), struct((vox, pair), BF16)),
        scratch_shapes=[
            pltpu.VMEM((vox, dim), BF16),
            pltpu.VMEM((vox, dim), BF16),
            pltpu.SemaphoreType.DMA((2,)),
        ],
        name="late",
        cost_estimate=pl.CostEstimate(flops=4 * width * dim * vox, bytes_accessed=4 * MIB, transcendentals=0),
        compiler_params=pltpu.CompilerParams(vmem_limit_bytes=8 * MIB),
    )(sent, terms, in_hbm(embed), in_hbm(head_t))

    sums = pl.pallas_call(
        functools.partial(backward_kernel, loss_weight, factor),
        in_specs=[vmem] * 9 + [hbm] + [vmem] * 2,
        out_specs=vmem,
        out_shape=struct((pair, width), F32),
        scratch_shapes=[
            pltpu.VMEM((width, rows), BF16),
            pltpu.VMEM((heads, keys, rows), BF16),
            pltpu.SemaphoreType.DMA((heads,)),
        ],
        name="backward",
        compiler_params=pltpu.CompilerParams(vmem_limit_bytes=BWD_MIB * MIB),
    )(part, other, held, mask, kept, own, at, c, inv, in_hbm(e), u, ut)

    mine, swapped = sum_over(sums, "seq")
    return pl.pallas_call(
        functools.partial(final_kernel, "seq"),
        out_shape=(struct((3, piece, width), F32), struct((piece, width), F32)),
        name="final",
        compiler_params=pltpu.CompilerParams(vmem_limit_bytes=8 * MIB),
    )(mine, swapped, terms, picked)


def solution(mesh):
    return jax.shard_map(
        per_device,
        mesh=mesh,
        in_specs=(P("seq", None), P("seq", None), P(), P(None, None, "head"), P(None, "head"), P()),
        out_specs=(P(None, "seq", "head"), P("seq", "head")),
        check_vma=False,
    )
```
